128 devices in a mesh: segment: 8 (over x, core), patch: 16 (over y, z).
Axes of the slice: x: 4, y: 4, z: 4, core: 2. Of those that a mesh axis runs over, the one named last changes fastest.
Arguments:
- latent: bfloat16 [2, 64, 64, 640], P(None, 'patch'), may hold values from -6 to 6
- stale_attn: bfloat16 [8, 2, 64, 64, 640], P('segment', None, 'patch'), may hold values from -6 to 6
- stale_edge: bfloat16 [8, 2, 32, 64, 640], P('segment', None, 'patch'), may hold values from -6 to 6
- norm_attn: float32 [8, 640], P('segment'), may hold values from 0.1 to 1.9
- query_w: bfloat16 [8, 640, 640], P('segment'), may hold values from -0.5 to 0.5
- key_w: bfloat16 [8, 640, 640], P('segment'), may hold values from -0.25 to 0.25
- value_w: bfloat16 [8, 640, 640], P('segment'), may hold values from -0.25 to 0.25
- out_w: bfloat16 [8, 640, 640], P('segment'), may hold values from -0.75 to 0.75
- norm_conv: float32 [8, 640], P('segment'), may hold values from 0.1 to 1.9
- conv_w: bfloat16 [8, 3, 3, 640, 640], P('segment'), may hold values from -0.078125 to 0.078125
Outputs:
- denoised: float32 [2, 64, 64, 640], P(None, 'patch', 'segment')
The draws below stay inside these ranges and needn't reach their ends.
All inputs are finite; a program needn't handle non-finite values.
Results may differ from the reference program's by a relative error of at most 0.035.
Values may be sent and summed in bfloat16 or wider, within the bound.
No kernel may reach another device: no remote copies, remote signals or barrier semaphores. Data moves between devices by JAX's collectives and lax.ppermute only.
A program may use at most 128 MiB of HBM per device.

```python
import jax
import jax.numpy as jnp
from jax import lax

C = 640
HEADS = 10
HD = 64
HR = 4
W = 64
M = 2
NB = 8
H = 64
N_PATCH = 16


def block_scale(key, dims, split, least, largest):
    level, own = 1.0, jax.random.fold_in(key, 6)
    for dim, blocks in split:
        heights = jnp.exp(jax.random.uniform(jax.random.fold_in(own, dim), (blocks,), jnp.float32, least / len(split), largest / len(split)))
        level = level * jnp.repeat(heights, dims[dim] // blocks).reshape([-1 if axis == dim else 1 for axis in range(len(dims))])
    return level


def noise(rng, extent, scale, limit, split=(), kind=jnp.bfloat16):
    entries = scale * jax.random.normal(rng, extent, jnp.float32)
    if split:
        entries = entries * block_scale(rng, extent, split, -0.22, 0.18)
    return jnp.clip(entries, -limit, limit).astype(kind)


def setup_inputs(seed: int = 0) -> dict:
    seeds = jax.random.split(jax.random.key(seed), 11)
    return {
        "latent": noise(seeds[0], (M, H, W, C), 1.0, 6.0, ((1, 16),)),
        "stale_attn": noise(seeds[1], (NB, M, H, W, C), 1.0, 6.0, ((0, 8), (2, 16))),
        "stale_edge": noise(seeds[2], (NB, M, 2 * N_PATCH, W, C), 1.0, 6.0, ((0, 8), (2, 16))),
        "norm_attn": jnp.clip(1.0 + 0.18 * jax.random.normal(seeds[3], (NB, C), jnp.float32), 0.1, 1.9),
        "query_w": noise(seeds[4], (NB, C, C), (C // 4) ** -0.5, 0.5, ((0, 8),)),
        "key_w": noise(seeds[5], (NB, C, C), C ** -0.5, 0.25, ((0, 8),)),
        "value_w": noise(seeds[6], (NB, C, C), C ** -0.5, 0.25, ((0, 8),)),
        "out_w": noise(seeds[7], (NB, C, C), HD ** -0.5, 0.75, ((0, 8),)),
        "norm_conv": jnp.clip(1.0 + 0.18 * jax.random.normal(seeds[8], (NB, C), jnp.float32), 0.1, 1.9),
        "conv_w": noise(seeds[9], (NB, 3, 3, C, C), (9 * C) ** -0.5, 0.078125, ((0, 8),)),
    }


def layer_norm(values, gain_vec):
    floats = values.astype(jnp.float32)
    center = floats - lax.optimization_barrier(jnp.mean(floats, axis=-1, keepdims=True))
    spread = lax.optimization_barrier(jnp.mean(center * center, axis=-1, keepdims=True))
    return center * lax.rsqrt(spread + 1e-05) * gain_vec

def project(row_data, weight):
    flattened = row_data.reshape(-1, row_data.shape[-1])
    result = jnp.dot(flattened, weight, preferred_element_type=jnp.float32).astype(jnp.bfloat16)
    return result.reshape(row_data.shape[:-1] + (weight.shape[1],))

def attend(queries, key_rows, value_rows):
    count = queries.shape[0]
    query_heads = queries.reshape(count, HEADS, HD).astype(jnp.float32)
    key_heads = key_rows.reshape(-1, HEADS, HD).astype(jnp.float32)
    value_heads = value_rows.reshape(-1, HEADS, HD).astype(jnp.float32)
    scores = jnp.einsum('qhd,khd->hqk', query_heads, key_heads) * HD ** (-0.5)
    exp_scores = jnp.exp(scores)
    totals = lax.optimization_barrier(jnp.sum(exp_scores, axis=-1))
    weights = exp_scores.astype(jnp.bfloat16).astype(jnp.float32)
    context = jnp.einsum('hqk,khd->qhd', weights, value_heads) / jnp.transpose(totals)[:, :, None]
    return context.reshape(count, HEADS * HD).astype(jnp.bfloat16)

def apply_block(current, stale_now, edge_now, gain_attn, query_weight, key_weight, value_weight, out_weight, gain_conv, kernel):
    cell_count = HR * W
    normed = layer_norm(current, gain_attn).astype(jnp.bfloat16)
    queries = project(normed, query_weight).reshape(N_PATCH, cell_count, C)
    fresh_key = project(normed, key_weight).reshape(N_PATCH, cell_count, C)
    fresh_value = project(normed, value_weight).reshape(N_PATCH, cell_count, C)
    stale_normed = layer_norm(stale_now, gain_attn).astype(jnp.bfloat16)
    stale_key = project(stale_normed, key_weight).reshape(N_PATCH, cell_count, C)
    stale_value = project(stale_normed, value_weight).reshape(N_PATCH, cell_count, C)
    patch_ids = jnp.arange(N_PATCH, dtype=jnp.int32)

    def per_patch(operands):
        patch_no, patch_queries = operands
        chosen = (patch_ids == patch_no)[:, None, None]
        key_set = jnp.where(chosen, fresh_key, stale_key).reshape(-1, C)
        value_set = jnp.where(chosen, fresh_value, stale_value).reshape(-1, C)
        return attend(patch_queries, key_set, value_set)
    context = lax.map(per_patch, (patch_ids, queries))
    attn_out = jnp.dot(context.reshape(-1, C), out_weight, preferred_element_type=jnp.float32)
    x_mid = current.astype(jnp.float32) + attn_out.reshape(H, W, C)
    conv_in = jax.nn.silu(layer_norm(x_mid, gain_conv)).astype(jnp.bfloat16)
    patched = conv_in.reshape(N_PATCH, HR, W, C)
    edge_pairs = edge_now.reshape(N_PATCH, 2, W, C)
    zero_row = jnp.zeros((1, W, C), jnp.bfloat16)
    above_rows = jnp.concatenate([zero_row, edge_pairs[:-1, 1]], 0)
    below_rows = jnp.concatenate([edge_pairs[1:, 0], zero_row], 0)
    extended = jnp.concatenate([above_rows[:, None], patched, below_rows[:, None]], 1)
    extended = jnp.pad(extended, ((0, 0), (0, 0), (1, 1), (0, 0)))
    conv_sum = jnp.zeros((H * W, C), jnp.float32)
    for row_tap in range(3):
        for col_tap in range(3):
            shifted = extended[:, row_tap:row_tap + HR, col_tap:col_tap + W].reshape(-1, C)
            conv_sum = conv_sum + jnp.dot(shifted, kernel[row_tap, col_tap], preferred_element_type=jnp.float32)
    return x_mid + conv_sum.reshape(H, W, C)

def reference(latent, stale_attn, stale_edge, norm_attn, query_w, key_w, value_w, out_w, norm_conv, conv_w):
    outputs = []
    for micro in range(M):
        current = latent[micro].astype(jnp.float32)
        for block_no in range(NB):
            current = apply_block(current, stale_attn[block_no, micro], stale_edge[block_no, micro], norm_attn[block_no], query_w[block_no], key_w[block_no], value_w[block_no], out_w[block_no], norm_conv[block_no], conv_w[block_no])
        outputs.append(current)
    return jnp.stack(outputs)
```

```python
import functools

import jax
import jax.numpy as jnp
from jax import lax
from jax.experimental import pallas as pl
from jax.experimental.pallas import tpu as pltpu
from jax.sharding import PartitionSpec as P

C = 640
PAIRS = 5
CELLS = 256
W = 64
KEYS = 4096
CHUNK = 1024
F32 = jnp.float32
BF = jnp.bfloat16
QSCALE = 0.125 * 1.4426950408889634


def normalize(values, gain):
    center = values - jnp.mean(values, axis=-1, keepdims=True)
    spread = jnp.mean(center * center, axis=-1, keepdims=True)
    return center * lax.rsqrt(spread + 1e-05) * gain


def dot(a, b):
    return jnp.dot(a, b, preferred_element_type=F32)


def dot_t(a, b):
    return lax.dot_general(a, b, (((1,), (1,)), ((), ())), preferred_element_type=F32)


def start_copy(use_own, own, other, target, sem):
    @pl.when(use_own)
    def _():
        pltpu.make_async_copy(own, target, sem).start()

    @pl.when(jnp.logical_not(use_own))
    def _():
        pltpu.make_async_copy(other, target, sem).start()


def wait_copy(own, target, sem):
    pltpu.make_async_copy(own, target, sem).wait()


def stale_kernel(
    block, raw_ref, ga_ref, wk_own, wv_own, wk_oth, wv_oth, kv_ref, wkv, sem
):
    @pl.when(pl.program_id(0) == 0)
    def _():
        use_own = lax.axis_index("segment") % 2 == block
        start_copy(use_own, wk_own, wk_oth, wkv.at[:, pl.ds(0, C)], sem.at[0])
        start_copy(use_own, wv_own, wv_oth, wkv.at[:, pl.ds(C, C)], sem.at[1])
        wait_copy(wk_own, wkv.at[:, pl.ds(0, C)], sem.at[0])
        wait_copy(wv_own, wkv.at[:, pl.ds(C, C)], sem.at[1])

    rows = raw_ref.shape[0] * raw_ref.shape[2]
    raw = raw_ref[...].reshape(rows, C).astype(F32)
    normed = normalize(raw, ga_ref[...]).astype(BF)
    out = dot(normed, wkv[...]).astype(BF)
    for part in range(2 * PAIRS):
        kv_ref[part] = out[:, part * 128 : (part + 1) * 128]


def stale_call(block, gathered, gain, own, other, patches=4):
    hbm = pl.BlockSpec(memory_space=pltpu.HBM)
    return pl.pallas_call(
        functools.partial(stale_kernel, block),
        grid=(16 // patches,),
        out_shape=jax.ShapeDtypeStruct((2 * PAIRS, KEYS, 128), BF),
        in_specs=[
            pl.BlockSpec((patches, 1, CELLS, C), lambda i: (i, block, 0, 0)),
            pl.BlockSpec((1, C), lambda i: (0, 0)),
            hbm,
            hbm,
            hbm,
            hbm,
        ],
        out_specs=pl.BlockSpec((2 * PAIRS, patches * CELLS, 128), lambda i: (0, i, 0)),
        scratch_shapes=[pltpu.VMEM((C, 2 * C), BF), pltpu.SemaphoreType.DMA((2,))],
        compiler_params=pltpu.CompilerParams(vmem_limit_bytes=40 << 20),
        cost_estimate=pl.CostEstimate(
            flops=4 * KEYS * C * C, transcendentals=0, bytes_accessed=6 * KEYS * C
        ),
        name="stale_%d" % block,
    )(gathered, gain, own["key"], own["value"], other["key"], other["value"])


NAMES = ("query", "key", "value", "out", "conv")


def block_kernel(block, *refs):
    x_ref, ga_ref, gc_ref, up_ref, dn_ref = refs[:5]
    own = dict(zip(NAMES, refs[5:10]))
    other = dict(zip(NAMES, refs[10:15]))
    kv_hbm, o_ref = refs[15:17]
    wqkv, wout, wconv, kv, queries, fresh, context, mid, cols, sem_w, sem_k = refs[17:]
    use_own = lax.axis_index("segment") % 2 == block
    targets = {
        "query": wqkv.at[:, pl.ds(0, C)],
        "key": wqkv.at[:, pl.ds(C, C)],
        "value": wqkv.at[:, pl.ds(2 * C, C)],
        "out": wout,
        "conv": wconv,
    }

    def start(name):
        start_copy(use_own, own[name], other[name], targets[name], sem_w.at[NAMES.index(name)])

    def wait(name):
        wait_copy(own[name], targets[name], sem_w.at[NAMES.index(name)])

    def part_copy(part):
        return pltpu.make_async_copy(kv_hbm.at[part], kv.at[part], sem_k.at[part])

    for name in NAMES[:3]:
        start(name)
    for pair in range(PAIRS):
        part_copy(pair).start()
        part_copy(PAIRS + pair).start()
    start("out")
    start("conv")

    x = x_ref[...].astype(F32)
    normed = normalize(x, ga_ref[...]).astype(BF)
    for name in NAMES[:3]:
        wait(name)
    made = dot(normed, wqkv[...])
    for pair in range(PAIRS):
        queries[pair] = (made[:, pair * 128 : (pair + 1) * 128] * QSCALE).astype(BF)
    for part in range(2 * PAIRS):
        fresh[part] = made[:, C + part * 128 : C + (part + 1) * 128].astype(BF)

    lane = lax.broadcasted_iota(jnp.int32, (CELLS, 128), 1)
    own_cells = pl.ds(pl.multiple_of(lax.axis_index("patch") * CELLS, CELLS), CELLS)

    def attend(pair, _):
        part_copy(pair).wait()
        part_copy(PAIRS + pair).wait()
        kv[pair, own_cells, :] = fresh[pair]
        kv[PAIRS + pair, own_cells, :] = fresh[PAIRS + pair]
        both = queries[pair]
        zero = jnp.zeros_like(both)
        heads = (jnp.where(lane < 64, both, zero), jnp.where(lane < 64, zero, both))
        totals = [jnp.zeros((CELLS, 128), F32)] * 2
        sums = [jnp.zeros((CELLS, 128), F32)] * 2
        for chunk in range(KEYS // CHUNK):
            cells = pl.ds(chunk * CHUNK, CHUNK)
            for head in range(2):
                weights = jnp.exp2(dot_t(heads[head], kv[pair, cells, :]))
                for tile in range(CHUNK // 128):
                    totals[head] = totals[head] + weights[:, tile * 128 : (tile + 1) * 128]
                sums[head] = sums[head] + dot(weights.astype(BF), kv[PAIRS + pair, cells, :])
        ready = [s / jnp.sum(t, axis=-1, keepdims=True) for s, t in zip(sums, totals)]
        context[pair] = jnp.where(lane < 64, ready[0], ready[1]).astype(BF)
        return 0

    lax.fori_loop(0, PAIRS, attend, 0)

    wait("out")
    x_mid = x_ref[...].astype(F32) + dot(
        jnp.concatenate([context[pair] for pair in range(PAIRS)], 1), wout[...]
    )
    mid[...] = x_mid
    gated = normalize(x_mid, gc_ref[...])
    gated = gated / (1.0 + jnp.exp(-gated))
    gated = gated.astype(BF).astype(F32)
    rows = CELLS + 2 * W
    extended = jnp.concatenate([up_ref[...].astype(F32), gated, dn_ref[...].astype(F32)], 0)
    col = lax.broadcasted_iota(jnp.int32, (rows, C), 0) % W
    cols[0] = jnp.where(col == 0, 0.0, pltpu.roll(extended, 1, 0)).astype(BF)
    cols[1] = extended.astype(BF)
    cols[2] = jnp.where(col == W - 1, 0.0, pltpu.roll(extended, rows - 1, 0)).astype(BF)
    wait("conv")
    total = mid[...]
    for i in range(3):
        for j in range(3):
            total = total + dot(cols[j, i * W : i * W + CELLS], wconv[3 * i + j])
    o_ref[...] = total.astype(o_ref.dtype)


def block_call(block, x, gain_attn, gain_conv, up, down, own, other, kv, out_dtype):
    vmem = pl.BlockSpec(memory_space=pltpu.VMEM)
    hbm = pl.BlockSpec(memory_space=pltpu.HBM)
    return pl.pallas_call(
        functools.partial(block_kernel, block),
        out_shape=jax.ShapeDtypeStruct((CELLS, C), out_dtype),
        in_specs=[vmem] * 5 + [hbm] * 11,
        out_specs=vmem,
        scratch_shapes=[
            pltpu.VMEM((C, 3 * C), BF),
            pltpu.VMEM((C, C), BF),
            pltpu.VMEM((9, C, C), BF),
            pltpu.VMEM((2 * PAIRS, KEYS, 128), BF),
            pltpu.VMEM((PAIRS, CELLS, 128), BF),
            pltpu.VMEM((2 * PAIRS, CELLS, 128), BF),
            pltpu.VMEM((PAIRS, CELLS, 128), BF),
            pltpu.VMEM((CELLS, C), F32),
            pltpu.VMEM((3, CELLS + 2 * W, C), BF),
            pltpu.SemaphoreType.DMA((5,)),
            pltpu.SemaphoreType.DMA((2 * PAIRS,)),
        ],
        compiler_params=pltpu.CompilerParams(vmem_limit_bytes=50 << 20),
        cost_estimate=pl.CostEstimate(
            flops=13_000_000_000, transcendentals=10_500_000, bytes_accessed=22_000_000
        ),
        name="block_%d" % block,
    )(
        x,
        gain_attn,
        gain_conv,
        up,
        down,
        *[own[name] for name in NAMES],
        *[other[name] for name in NAMES],
        kv,
    )


def shards(
    latent, stale_attn, stale_edge, norm_attn, query_w, key_w, value_w, out_w, norm_conv, conv_w
):
    core = lax.axis_index("segment") % 2
    is_first = core == 0
    sibling = [(i, i ^ 1) for i in range(8)]

    def swap(value):
        return lax.ppermute(value, "segment", sibling)

    def ordered(own, other):
        return jnp.where(is_first, own, other), jnp.where(is_first, other, own)

    def exchanged(value):
        keep = lax.dynamic_index_in_dim(value, core, 0, keepdims=False)
        give = lax.dynamic_index_in_dim(value, 1 - core, 0, keepdims=False)
        return ordered(keep, swap(give))

    raw = jnp.stack(exchanged(stale_attn[0].reshape(2, CELLS, C)))
    gathered = lax.all_gather(raw, "patch", axis=0)

    edges = jnp.stack(exchanged(stale_edge[0]))
    upper = lax.ppermute(edges[:, 1], "patch", [(i, i + 1) for i in range(15)])
    lower = lax.ppermute(edges[:, 0], "patch", [(i + 1, i) for i in range(15)])

    own = {
        "query": query_w[0],
        "key": key_w[0],
        "value": value_w[0],
        "out": out_w[0],
        "conv": conv_w[0].reshape(9, C, C),
    }
    other = {name: swap(own[name]) for name in ("key", "value", "query", "out", "conv")}
    gains = ordered(norm_attn, swap(norm_attn))
    conv_gains = ordered(norm_conv, swap(norm_conv))

    stored = [stale_call(b, gathered, gains[b], own, other) for b in range(2)]
    x = lax.dynamic_index_in_dim(latent, core, 0, keepdims=False).reshape(CELLS, C)
    for stage in range(4):
        if stage:
            x = lax.ppermute(x, "segment", [(i, i + 2) for i in range(6)])
        for b in range(2):
            x = block_call(
                b, x, gains[b], conv_gains[b], upper[b], lower[b], own, other, stored[b],
                BF if b else F32,
            )

    groups = x.reshape(4, 4, 2, 8, C)
    keep = lax.dynamic_index_in_dim(groups, core, 2, keepdims=False)
    got = swap(lax.dynamic_index_in_dim(groups, 1 - core, 2, keepdims=False))
    both = jnp.stack(ordered(keep, got))
    result = jnp.where(lax.axis_index("segment") >= 6, both[:, :, 3], jnp.zeros_like(both[:, :, 3]))
    for d in (1, 2, 3):
        result = result + lax.ppermute(
            both[:, :, (3 + d) % 4], "segment", [(6, (6 + 2 * d) % 8), (7, (7 + 2 * d) % 8)]
        )
    return result.astype(F32)


def solution(mesh):
    in_specs = (
        P(None, "patch", None, None),
        P("segment", None, "patch", None, None),
        P("segment", None, "patch", None, None),
        P("segment", None),
        P("segment", None, None),
        P("segment", None, None),
        P("segment", None, None),
        P("segment", None, None),
        P("segment", None),
        P("segment", None, None, None, None),
    )
    out_specs = P(None, "patch", "segment", None)
    return jax.shard_map(shards, mesh=mesh, in_specs=in_specs, out_specs=out_specs, check_vma=False)
```

```python
import functools

import jax
import jax.numpy as jnp
from jax import lax
from jax.experimental import pallas as pl
from jax.experimental.pallas import tpu as pltpu
from jax.sharding import PartitionSpec as P

C = 640
PAIRS = 5
CELLS = 256
W = 64
KEYS = 4096
CHUNK = 1024
F32 = jnp.float32
BF = jnp.bfloat16
QSCALE = 0.125 * 1.4426950408889634


def normalize(values, gain):
    center = values - jnp.mean(values, axis=-1, keepdims=True)
    spread = jnp.mean(center * center, axis=-1, keepdims=True)
    return center * lax.rsqrt(spread + 1e-05) * gain


def dot(a, b):
    return jnp.dot(a, b, preferred_element_type=F32)


def dot_t(a, b):
    return lax.dot_general(a, b, (((1,), (1,)), ((), ())), preferred_element_type=F32)


def start_copy(use_own, own, other, target, sem):
    @pl.when(use_own)
    def _():
        pltpu.make_async_copy(own, target, sem).start()

    @pl.when(jnp.logical_not(use_own))
    def _():
        pltpu.make_async_copy(other, target, sem).start()


def wait_copy(own, target, sem):
    pltpu.make_async_copy(own, target, sem).wait()


def stale_kernel(count, *refs):
    pieces, (ga_ref, wkv_ref, kv_ref) = refs[:count], refs[count:]
    block, piece = pl.program_id(0), pl.program_id(1)
    raw = pieces[0][...]
    for i in range(1, count):
        raw = jnp.where(piece == i, pieces[i][...], raw)
    raw = raw.reshape(-1, C).astype(F32)
    normed = normalize(raw, ga_ref[pl.ds(block, 1), :]).astype(BF)
    out = dot(normed, wkv_ref[...]).astype(BF)
    for part in range(2 * PAIRS):
        kv_ref[part] = out[:, part * 128 : (part + 1) * 128]


def stale_call(pieces, gains, wkv, patches=2):
    count, size = len(pieces), pieces[0].shape[0]
    steps = size // patches

    def piece_spec(i):
        def place(b, piece, step):
            return jnp.where(piece == i, step, jnp.where(piece < i, 0, steps - 1)), b, 0, 0

        return pl.BlockSpec((patches, None, CELLS, C), place)

    return pl.pallas_call(
        functools.partial(stale_kernel, count),
        grid=(2, count, steps),
        out_shape=jax.ShapeDtypeStruct((2, 2 * PAIRS, count * size * CELLS, 128), BF),
        in_specs=[piece_spec(i) for i in range(count)]
        + [
            pl.BlockSpec((2, C), lambda b, piece, step: (0, 0)),
            pl.BlockSpec((None, C, 2 * C), lambda b, piece, step: (b, 0, 0)),
        ],
        out_specs=pl.BlockSpec(
            (None, 2 * PAIRS, patches * CELLS, 128),
            lambda b, piece, step: (b, 0, piece * steps + step, 0),
        ),
        compiler_params=pltpu.CompilerParams(vmem_limit_bytes=50 << 20),
        cost_estimate=pl.CostEstimate(
            flops=8 * count * size * CELLS * C * C,
            transcendentals=0,
            bytes_accessed=12 * count * size * CELLS * C,
        ),
        name="stale_%d" % (count * size),
    )(*pieces, gains, wkv)


STORES = 3
NAMES = ("query", "key", "value", "out", "conv")


def block_kernel(*refs):
    x_ref, ga_ref, gc_ref, up_ref, dn_ref = refs[:5]
    own = dict(zip(NAMES, refs[5:10]))
    other = dict(zip(NAMES, refs[10:15]))
    kv_hbm, refs = refs[15 : 15 + STORES], refs[15 + STORES :]
    o_ref, wqkv, wout, wconv, kv, queries, fresh, context, mid, cols, sem_w, sem_k = refs
    core = lax.axis_index("segment") % 2
    targets = {
        "query": wqkv.at[:, pl.ds(0, C)],
        "key": wqkv.at[:, pl.ds(C, C)],
        "value": wqkv.at[:, pl.ds(2 * C, C)],
        "out": wout,
        "conv": wconv,
    }

    def start(place, *names):
        for name in names:
            start_copy(
                core == place,
                own[name],
                other[name],
                targets[name],
                sem_w.at[NAMES.index(name)],
            )

    def wait(name):
        wait_copy(own[name], targets[name], sem_w.at[NAMES.index(name)])

    def pair_copies(place, pair):
        copies = []
        for part in (pair, PAIRS + pair):
            begin = 0
            for i, store in enumerate(kv_hbm):
                cells = pl.ds(begin, store.shape[2])
                begin += store.shape[2]
                copies.append(
                    pltpu.make_async_copy(
                        store.at[place, part], kv.at[part, cells], sem_k.at[part, i]
                    )
                )
        return copies

    start(0, "query", "key", "value")
    for pair in range(PAIRS):
        for copy in pair_copies(0, pair):
            copy.start()
    start(0, "out", "conv")
    mid[...] = x_ref[...].astype(F32)
    lane = lax.broadcasted_iota(jnp.int32, (CELLS, 128), 1)
    own_cells = pl.ds(0, CELLS)

    def one_block(place, _):
        def ahead(work):
            pl.when(place == 0)(work)

        normed = normalize(mid[...], ga_ref[pl.ds(place, 1), :]).astype(BF)
        for name in NAMES[:3]:
            wait(name)
        made = dot(normed, wqkv[...])
        for pair in range(PAIRS):
            queries[pair] = (made[:, pair * 128 : (pair + 1) * 128] * QSCALE).astype(BF)
        for part in range(2 * PAIRS):
            fresh[part] = made[:, C + part * 128 : C + (part + 1) * 128].astype(BF)
        ahead(lambda: start(1, "query", "key", "value"))

        def attend(pair):
            for copy in pair_copies(0, pair):
                copy.wait()
            kv[pair, own_cells, :] = fresh[pair]
            kv[PAIRS + pair, own_cells, :] = fresh[PAIRS + pair]
            both = queries[pair]
            zero = jnp.zeros_like(both)
            heads = (jnp.where(lane < 64, both, zero), jnp.where(lane < 64, zero, both))
            totals = [jnp.zeros((CELLS, 128), F32)] * 2
            sums = [jnp.zeros((CELLS, 128), F32)] * 2
            for chunk in range(KEYS // CHUNK):
                cells = pl.ds(chunk * CHUNK, CHUNK)
                for head in range(2):
                    weights = jnp.exp2(dot_t(heads[head], kv[pair, cells, :]))
                    for tile in range(CHUNK // 128):
                        totals[head] = totals[head] + weights[:, tile * 128 : (tile + 1) * 128]
                    sums[head] = sums[head] + dot(weights.astype(BF), kv[PAIRS + pair, cells, :])
            ready = [s / jnp.sum(t, axis=-1, keepdims=True) for s, t in zip(sums, totals)]
            context[pair] = jnp.where(lane < 64, ready[0], ready[1]).astype(BF)

            def next_pair():
                for copy in pair_copies(1, pair):
                    copy.start()

            ahead(next_pair)

        for pair in range(PAIRS):
            attend(pair)

        wait("out")
        x_mid = mid[...] + dot(
            jnp.concatenate([context[pair] for pair in range(PAIRS)], 1), wout[...]
        )
        mid[...] = x_mid
        ahead(lambda: start(1, "out"))
        gated = normalize(x_mid, gc_ref[pl.ds(place, 1), :])
        gated = gated / (1.0 + jnp.exp(-gated))
        gated = gated.astype(BF).astype(F32)
        rows = CELLS + 2 * W
        extended = jnp.concatenate(
            [up_ref[place].astype(F32), gated, dn_ref[place].astype(F32)], 0
        )
        col = lax.broadcasted_iota(jnp.int32, (rows, C), 0) % W
        cols[0] = jnp.where(col == 0, 0.0, pltpu.roll(extended, 1, 0)).astype(BF)
        cols[1] = extended.astype(BF)
        cols[2] = jnp.where(col == W - 1, 0.0, pltpu.roll(extended, rows - 1, 0)).astype(BF)
        wait("conv")

        def tap_row(i, _):
            cells = pl.ds(pl.multiple_of(i * W, W), CELLS)
            total = mid[...]
            for j in range(3):
                total = total + dot(cols[j, cells, :], wconv[3 * i + j])
            mid[...] = total
            return 0

        lax.fori_loop(0, 3, tap_row, 0)
        ahead(lambda: start(1, "conv"))
        return 0

    lax.fori_loop(0, 2, one_block, 0)
    o_ref[...] = mid[...].astype(o_ref.dtype)


def block_call(x, gain_attn, gain_conv, up, down, own, other, stored):
    vmem = pl.BlockSpec(memory_space=pltpu.VMEM)
    hbm = pl.BlockSpec(memory_space=pltpu.HBM)
    return pl.pallas_call(
        block_kernel,
        out_shape=jax.ShapeDtypeStruct((CELLS, C), BF),
        in_specs=[vmem] * 5 + [hbm] * (10 + STORES),
        out_specs=vmem,
        scratch_shapes=[
            pltpu.VMEM((C, 3 * C), BF),
            pltpu.VMEM((C, C), BF),
            pltpu.VMEM((9, C, C), BF),
            pltpu.VMEM((2 * PAIRS, KEYS, 128), BF),
            pltpu.VMEM((PAIRS, CELLS, 128), BF),
            pltpu.VMEM((2 * PAIRS, CELLS, 128), BF),
            pltpu.VMEM((PAIRS, CELLS, 128), BF),
            pltpu.VMEM((CELLS, C), F32),
            pltpu.VMEM((3, CELLS + 2 * W, C), BF),
            pltpu.SemaphoreType.DMA((5,)),
            pltpu.SemaphoreType.DMA((2 * PAIRS, STORES)),
        ],
        compiler_params=pltpu.CompilerParams(vmem_limit_bytes=58 << 20),
        cost_estimate=pl.CostEstimate(
            flops=2 * 13_000_000_000,
            transcendentals=2 * 10_500_000,
            bytes_accessed=2 * 22_000_000,
        ),
        name="blocks",
    )(
        x,
        gain_attn,
        gain_conv,
        up,
        down,
        *[own[name] for name in NAMES],
        *[other[name] for name in NAMES],
        *stored,
    )


def turned(value, leg, by):
    pairs = []
    for segment in range(8):
        for y in range(4):
            for z in range(4):
                if segment % 2 == leg:
                    to = y, (z + by) % 4
                else:
                    to = (y + by) % 4, z
                pairs.append((16 * segment + 4 * y + z, 16 * segment + 4 * to[0] + to[1]))
    return lax.ppermute(value, ("segment", "patch"), pairs)


def ring_near(value, leg):
    return turned(value, leg, 1), turned(value, leg, -1)


def ring_far(back, ahead, leg):
    half = back.shape[0] // 2
    return turned(back[:half], leg, 1), turned(ahead[half:], leg, -1)


def shards(
    latent, stale_attn, stale_edge, norm_attn, query_w, key_w, value_w, out_w, norm_conv, conv_w
):
    core = lax.axis_index("segment") % 2
    is_first = core == 0
    sibling = [(i, i ^ 1) for i in range(8)]

    def swap(value):
        return lax.ppermute(value, "segment", sibling)

    def ordered(own, other):
        return jnp.where(is_first, own, other), jnp.where(is_first, other, own)

    def exchanged(value):
        keep = lax.dynamic_index_in_dim(value, core, 0, keepdims=False)
        give = lax.dynamic_index_in_dim(value, 1 - core, 0, keepdims=False)
        return ordered(keep, swap(give))

    raw = jnp.stack(exchanged(stale_attn[0].reshape(2, CELLS, C)))
    back, ahead = ring_near(raw, 0)
    far = ring_far(back, ahead, 0)
    row = jnp.stack([raw, back, jnp.concatenate(far, 0), ahead])
    back, ahead = ring_near(row, 1)
    far = ring_far(back, ahead, 1)

    edges = jnp.stack(exchanged(stale_edge[0]))
    upper = lax.ppermute(edges[:, 1], "patch", [(i, i + 1) for i in range(15)])
    lower = lax.ppermute(edges[:, 0], "patch", [(i + 1, i) for i in range(15)])

    own = dict(zip(NAMES, (query_w[0], key_w[0], value_w[0], out_w[0], conv_w[0].reshape(9, C, C))))
    other = {name: swap(own[name]) for name in ("key", "value", "query", "out", "conv")}
    gains = jnp.concatenate(ordered(norm_attn, swap(norm_attn)), 0)
    conv_gains = jnp.concatenate(ordered(norm_conv, swap(norm_conv)), 0)

    x = lax.dynamic_index_in_dim(latent, core, 0, keepdims=False).reshape(CELLS, C)
    wkv = jnp.stack(
        ordered(*[jnp.concatenate([w["key"], w["value"]], 1) for w in (own, other)])
    )
    stored = [stale_call(pieces, gains, wkv) for pieces in ([row], [back, ahead], far)]

    def two_blocks(x):
        return block_call(x, gains, conv_gains, upper, lower, own, other, stored)

    def hop(x):
        return lax.ppermute(x, "segment", [(i, i + 2) for i in range(6)])

    def chip_stage(stage, x):
        return lax.cond(stage < 3, hop, lambda x: x, two_blocks(x))

    x = lax.fori_loop(0, 4, chip_stage, x)

    groups = x.reshape(4, 4, 2, 8, C)
    keep = lax.dynamic_index_in_dim(groups, core, 2, keepdims=False)
    got = swap(lax.dynamic_index_in_dim(groups, 1 - core, 2, keepdims=False))
    both = jnp.stack(ordered(keep, got))
    result = jnp.where(lax.axis_index("segment") >= 6, both[:, :, 3], jnp.zeros_like(both[:, :, 3]))
    for d in (1, 2, 3):
        result = result + lax.ppermute(
            both[:, :, (3 + d) % 4], "segment", [(6, (6 + 2 * d) % 8), (7, (7 + 2 * d) % 8)]
        )
    return result.astype(F32)


def solution(mesh):
    in_specs = (
        P(None, "patch", None, None),
        P("segment", None, "patch", None, None),
        P("segment", None, "patch", None, None),
        P("segment", None),
        P("segment", None, None),
        P("segment", None, None),
        P("segment", None, None),
        P("segment", None, None),
        P("segment", None),
        P("segment", None, None, None, None),
    )
    out_specs = P(None, "patch", "segment", None)
    return jax.shard_map(shards, mesh=mesh, in_specs=in_specs, out_specs=out_specs, check_vma=False)
```

```python
import functools

import jax
import jax.numpy as jnp
from jax import lax
from jax.experimental import pallas as pl
from jax.experimental.pallas import tpu as pltpu
from jax.sharding import PartitionSpec as P

C = 640
PAIRS = 5
CELLS = 256
W = 64
KEYS = 4096
CHUNK = 1024
F32 = jnp.float32
BF = jnp.bfloat16
QSCALE = 0.125 * 1.4426950408889634


def normalize(values, gain):
    center = values - jnp.mean(values, axis=-1, keepdims=True)
    spread = jnp.mean(center * center, axis=-1, keepdims=True)
    return center * lax.rsqrt(spread + 1e-05) * gain


def dot(a, b):
    return jnp.dot(a, b, preferred_element_type=F32)


def dot_t(a, b):
    return lax.dot_general(a, b, (((1,), (1,)), ((), ())), preferred_element_type=F32)


def start_copy(use_own, own, other, target, sem):
    @pl.when(use_own)
    def _():
        pltpu.make_async_copy(own, target, sem).start()

    @pl.when(jnp.logical_not(use_own))
    def _():
        pltpu.make_async_copy(other, target, sem).start()


def wait_copy(own, target, sem):
    pltpu.make_async_copy(own, target, sem).wait()


def stale_kernel(count, *refs):
    pieces, (ga_ref, wkv_ref, kv_ref) = refs[:count], refs[count:]
    block, piece = pl.program_id(0), pl.program_id(1)
    raw = pieces[0][...]
    for i in range(1, count):
        raw = jnp.where(piece == i, pieces[i][...], raw)
    raw = raw.reshape(-1, C).astype(F32)
    normed = normalize(raw, ga_ref[pl.ds(block, 1), :]).astype(BF)
    out = dot(normed, wkv_ref[...]).astype(BF)
    for part in range(2 * PAIRS):
        kv_ref[part] = out[:, part * 128 : (part + 1) * 128]


def stale_call(pieces, gains, wkv):
    count, size = len(pieces), pieces[0].shape[0]
    patches = min(size, 4)
    steps = size // patches

    def piece_spec(i):
        def place(b, piece, step):
            return jnp.where(piece == i, step, jnp.where(piece < i, 0, steps - 1)), b, 0, 0

        return pl.BlockSpec((patches, None, CELLS, C), place)

    return pl.pallas_call(
        functools.partial(stale_kernel, count),
        grid=(2, count, steps),
        out_shape=jax.ShapeDtypeStruct((2, 2 * PAIRS, count * size * CELLS, 128), BF),
        in_specs=[piece_spec(i) for i in range(count)]
        + [
            pl.BlockSpec((2, C), lambda b, piece, step: (0, 0)),
            pl.BlockSpec((None, C, 2 * C), lambda b, piece, step: (b, 0, 0)),
        ],
        out_specs=pl.BlockSpec(
            (None, 2 * PAIRS, patches * CELLS, 128),
            lambda b, piece, step: (b, 0, piece * steps + step, 0),
        ),
        compiler_params=pltpu.CompilerParams(vmem_limit_bytes=50 << 20),
        cost_estimate=pl.CostEstimate(
            flops=8 * count * size * CELLS * C * C,
            transcendentals=0,
            bytes_accessed=12 * count * size * CELLS * C,
        ),
        name="stale_%d" % (count * size),
    )(*pieces, gains, wkv)


STORES = 3
NAMES = ("query", "key", "value", "out", "conv")


def block_kernel(*refs):
    x_ref, ga_ref, gc_ref, up_ref, dn_ref = refs[:5]
    own = dict(zip(NAMES, refs[5:10]))
    other = dict(zip(NAMES, refs[10:15]))
    kv_hbm, refs = refs[15 : 15 + STORES], refs[15 + STORES :]
    o_ref, wqkv, wout, wconv, kv, queries, fresh, context, mid, cols, sem_w, sem_k = refs
    core = lax.axis_index("segment") % 2
    targets = {
        "query": wqkv.at[:, pl.ds(0, C)],
        "key": wqkv.at[:, pl.ds(C, C)],
        "value": wqkv.at[:, pl.ds(2 * C, C)],
        "out": wout,
        "conv": wconv,
    }

    def start(place, *names):
        for name in names:
            start_copy(
                core == place,
                own[name],
                other[name],
                targets[name],
                sem_w.at[NAMES.index(name)],
            )

    def wait(name):
        wait_copy(own[name], targets[name], sem_w.at[NAMES.index(name)])

    def pair_copies(place, pair):
        copies = []
        for part in (pair, PAIRS + pair):
            begin = 0
            for i, store in enumerate(kv_hbm):
                cells = pl.ds(begin, store.shape[2])
                begin += store.shape[2]
                copies.append(
                    pltpu.make_async_copy(
                        store.at[place, part], kv.at[part, cells], sem_k.at[part, i]
                    )
                )
        return copies

    start(0, "query", "key", "value")
    mid[...] = x_ref[...].astype(F32)
    lane = lax.broadcasted_iota(jnp.int32, (CELLS, 128), 1)
    own_cells = pl.ds(0, CELLS)

    def one_block(place, _):
        def ahead(work):
            pl.when(place == 0)(work)

        normed = normalize(mid[...], ga_ref[pl.ds(place, 1), :]).astype(BF)
        for name in NAMES[:3]:
            wait(name)

        @pl.when(place == 0)
        def _():
            for pair in range(PAIRS):
                for copy in pair_copies(0, pair):
                    copy.start()
            start(0, "out", "conv")

        made = dot(normed, wqkv[...])
        for pair in range(PAIRS):
            queries[pair] = (made[:, pair * 128 : (pair + 1) * 128] * QSCALE).astype(BF)
        for part in range(2 * PAIRS):
            fresh[part] = made[:, C + part * 128 : C + (part + 1) * 128].astype(BF)
        ahead(lambda: start(1, "query", "key", "value"))

        def attend(pair):
            for copy in pair_copies(0, pair):
                copy.wait()
            kv[pair, own_cells, :] = fresh[pair]
            kv[PAIRS + pair, own_cells, :] = fresh[PAIRS + pair]
            both = queries[pair]
            zero = jnp.zeros_like(both)
            heads = (jnp.where(lane < 64, both, zero), jnp.where(lane < 64, zero, both))
            totals = [jnp.zeros((CELLS, 128), F32)] * 2
            sums = [jnp.zeros((CELLS, 128), F32)] * 2
            for chunk in range(KEYS // CHUNK):
                cells = pl.ds(chunk * CHUNK, CHUNK)
                for head in range(2):
                    weights = jnp.exp2(dot_t(heads[head], kv[pair, cells, :]))
                    for tile in range(CHUNK // 128):
                        totals[head] = totals[head] + weights[:, tile * 128 : (tile + 1) * 128]
                    sums[head] = sums[head] + dot(weights.astype(BF), kv[PAIRS + pair, cells, :])
            ready = [s / jnp.sum(t, axis=-1, keepdims=True) for s, t in zip(sums, totals)]
            context[pair] = jnp.where(lane < 64, ready[0], ready[1]).astype(BF)

            def next_pair():
                for copy in pair_copies(1, pair):
                    copy.start()

            ahead(next_pair)

        for pair in range(PAIRS):
            attend(pair)

        wait("out")
        x_mid = mid[...] + dot(
            jnp.concatenate([context[pair] for pair in range(PAIRS)], 1), wout[...]
        )
        mid[...] = x_mid
        ahead(lambda: start(1, "out"))
        gated = normalize(x_mid, gc_ref[pl.ds(place, 1), :])
        gated = gated / (1.0 + jnp.exp(-gated))
        gated = gated.astype(BF).astype(F32)
        rows = CELLS + 2 * W
        extended = jnp.concatenate(
            [up_ref[place].astype(F32), gated, dn_ref[place].astype(F32)], 0
        )
        col = lax.broadcasted_iota(jnp.int32, (rows, C), 0) % W
        cols[0] = jnp.where(col == 0, 0.0, pltpu.roll(extended, 1, 0)).astype(BF)
        cols[1] = extended.astype(BF)
        cols[2] = jnp.where(col == W - 1, 0.0, pltpu.roll(extended, rows - 1, 0)).astype(BF)
        wait("conv")

        def tap_row(i, _):
            cells = pl.ds(pl.multiple_of(i * W, W), CELLS)
            total = mid[...]
            for j in range(3):
                total = total + dot(cols[j, cells, :], wconv[3 * i + j])
            mid[...] = total
            return 0

        lax.fori_loop(0, 3, tap_row, 0)
        ahead(lambda: start(1, "conv"))
        return 0

    lax.fori_loop(0, 2, one_block, 0)
    o_ref[...] = mid[...].astype(o_ref.dtype)


def block_call(x, gain_attn, gain_conv, up, down, own, other, stored):
    vmem = pl.BlockSpec(memory_space=pltpu.VMEM)
    hbm = pl.BlockSpec(memory_space=pltpu.HBM)
    return pl.pallas_call(
        block_kernel,
        out_shape=jax.ShapeDtypeStruct((CELLS, C), BF),
        in_specs=[vmem] * 5 + [hbm] * (10 + STORES),
        out_specs=vmem,
        scratch_shapes=[
            pltpu.VMEM((C, 3 * C), BF),
            pltpu.VMEM((C, C), BF),
            pltpu.VMEM((9, C, C), BF),
            pltpu.VMEM((2 * PAIRS, KEYS, 128), BF),
            pltpu.VMEM((PAIRS, CELLS, 128), BF),
            pltpu.VMEM((2 * PAIRS, CELLS, 128), BF),
            pltpu.VMEM((PAIRS, CELLS, 128), BF),
            pltpu.VMEM((CELLS, C), F32),
            pltpu.VMEM((3, CELLS + 2 * W, C), BF),
            pltpu.SemaphoreType.DMA((5,)),
            pltpu.SemaphoreType.DMA((2 * PAIRS, STORES)),
        ],
        compiler_params=pltpu.CompilerParams(vmem_limit_bytes=58 << 20),
        cost_estimate=pl.CostEstimate(
            flops=2 * 13_000_000_000,
            transcendentals=2 * 10_500_000,
            bytes_accessed=2 * 22_000_000,
        ),
        name="blocks",
    )(
        x,
        gain_attn,
        gain_conv,
        up,
        down,
        *[own[name] for name in NAMES],
        *[other[name] for name in NAMES],
        *stored,
    )


def turned(value, leg, by):
    pairs = []
    for segment in range(8):
        for y in range(4):
            for z in range(4):
                if segment % 2 == leg:
                    to = y, (z + by) % 4
                else:
                    to = (y + by) % 4, z
                pairs.append((16 * segment + 4 * y + z, 16 * segment + 4 * to[0] + to[1]))
    return lax.ppermute(value, ("segment", "patch"), pairs)


def ring_near(value, leg):
    return turned(value, leg, 1), turned(value, leg, -1)


def ring_far(back, ahead, leg):
    half = back.shape[0] // 2
    return turned(back[:half], leg, 1), turned(ahead[half:], leg, -1)


def shards(
    latent, stale_attn, stale_edge, norm_attn, query_w, key_w, value_w, out_w, norm_conv, conv_w
):
    core = lax.axis_index("segment") % 2
    is_first = core == 0
    sibling = [(i, i ^ 1) for i in range(8)]

    def swap(value):
        return lax.ppermute(value, "segment", sibling)

    def ordered(own, other):
        return jnp.where(is_first, own, other), jnp.where(is_first, other, own)

    def exchanged(value):
        keep = lax.dynamic_index_in_dim(value, core, 0, keepdims=False)
        give = lax.dynamic_index_in_dim(value, 1 - core, 0, keepdims=False)
        return ordered(keep, swap(give))

    own = dict(zip(NAMES, (query_w[0], key_w[0], value_w[0], out_w[0], conv_w[0].reshape(9, C, C))))
    mine = jnp.concatenate(
        [stale_attn[0].reshape(2, CELLS, C), stale_edge[0].reshape(2, 2 * W, C)], 1
    )
    mine = jnp.stack(exchanged(mine))
    raw, edges = mine[:, :CELLS], mine[:, CELLS:].reshape(2, 2, W, C)
    raw, first_sent, norm_attn = lax.optimization_barrier(
        (raw, {name: own[name] for name in ("key", "value")}, norm_attn)
    )
    other = {name: swap(value) for name, value in first_sent.items()}
    gains = jnp.concatenate(ordered(norm_attn, swap(norm_attn)), 0)
    wkv = jnp.stack(
        ordered(*[jnp.concatenate([w["key"], w["value"]], 1) for w in (own, other)])
    )
    back, ahead = ring_near(raw, 0)
    far = ring_far(back, ahead, 0)
    row = jnp.stack([raw, back, jnp.concatenate(far, 0), ahead])
    row, sent, edges, norm_conv = lax.optimization_barrier(
        (row, {name: own[name] for name in ("query", "out", "conv")}, edges, norm_conv)
    )
    back, ahead = ring_near(row, 1)
    upper = lax.ppermute(edges[:, 1], "patch", [(i, i + 1) for i in range(15)])
    lower = lax.ppermute(edges[:, 0], "patch", [(i + 1, i) for i in range(15)])
    stored = stale_call([row], gains, wkv)
    back, ahead, upper, lower, stored = lax.optimization_barrier(
        (back, ahead, upper, lower, stored)
    )
    far = ring_far(back, ahead, 1)

    other |= {name: swap(value) for name, value in sent.items()}
    conv_gains = jnp.concatenate(ordered(norm_conv, swap(norm_conv)), 0)

    x = lax.dynamic_index_in_dim(latent, core, 0, keepdims=False).reshape(CELLS, C)
    stored = [stored] + [stale_call(pieces, gains, wkv) for pieces in ([back, ahead], far)]

    def two_blocks(x):
        return block_call(x, gains, conv_gains, upper, lower, own, other, stored)

    def hop(x):
        return lax.ppermute(x, "segment", [(i, i + 2) for i in range(6)])

    def chip_stage(stage, x):
        return lax.cond(stage < 3, hop, lambda x: x, two_blocks(x))

    x = lax.fori_loop(0, 4, chip_stage, x)

    groups = x.reshape(4, 4, 2, 8, C)
    keep = lax.dynamic_index_in_dim(groups, core, 2, keepdims=False)
    got = swap(lax.dynamic_index_in_dim(groups, 1 - core, 2, keepdims=False))
    both = jnp.stack(ordered(keep, got))
    result = jnp.where(lax.axis_index("segment") >= 6, both[:, :, 3], jnp.zeros_like(both[:, :, 3]))
    for d in (1, 2, 3):
        result = result + lax.ppermute(
            both[:, :, (3 + d) % 4], "segment", [(6, (6 + 2 * d) % 8), (7, (7 + 2 * d) % 8)]
        )
    return result.astype(F32)


def solution(mesh):
    in_specs = (
        P(None, "patch", None, None),
        P("segment", None, "patch", None, None),
        P("segment", None, "patch", None, None),
        P("segment", None),
        P("segment", None, None),
        P("segment", None, None),
        P("segment", None, None),
        P("segment", None, None),
        P("segment", None),
        P("segment", None, None, None, None),
    )
    out_specs = P(None, "patch", "segment", None)
    return jax.shard_map(shards, mesh=mesh, in_specs=in_specs, out_specs=out_specs, check_vma=False)
```

```python
import functools

import jax
import jax.numpy as jnp
from jax import lax
from jax.experimental import pallas as pl
from jax.experimental.pallas import tpu as pltpu
from jax.sharding import PartitionSpec as P

C = 640
PAIRS = 5
CELLS = 256
W = 64
KEYS = 4096
CHUNK = 2048
F32 = jnp.float32
BF = jnp.bfloat16
QSCALE = 0.125 * 1.4426950408889634


def normalize(values, gain):
    center = values - jnp.mean(values, axis=-1, keepdims=True)
    spread = jnp.mean(center * center, axis=-1, keepdims=True)
    return center * lax.rsqrt(spread + 1e-05) * gain


def dot(a, b):
    return jnp.dot(a, b, preferred_element_type=F32)


def dot_t(a, b):
    return lax.dot_general(a, b, (((1,), (1,)), ((), ())), preferred_element_type=F32)


def dot_turned(a, b):
    return lax.dot_general(a, b, (((0,), (1,)), ((), ())), preferred_element_type=F32)


def start_copy(use_own, own, other, target, sem):
    @pl.when(use_own)
    def _():
        pltpu.make_async_copy(own, target, sem).start()

    @pl.when(jnp.logical_not(use_own))
    def _():
        pltpu.make_async_copy(other, target, sem).start()


def wait_copy(own, target, sem):
    pltpu.make_async_copy(own, target, sem).wait()


def stale_kernel(count, *refs):
    pieces, (ga_ref, wk_ref, wv_ref, k_ref, vt_ref) = refs[:count], refs[count:]
    block, piece = pl.program_id(0), pl.program_id(1)
    raw = pieces[0][...]
    for i in range(1, count):
        raw = jnp.where(piece == i, pieces[i][...], raw)
    raw = raw.reshape(-1, C).astype(F32)
    normed = normalize(raw, ga_ref[pl.ds(block, 1), :]).astype(BF)
    keys = dot(normed, wk_ref[...]).astype(BF)
    values = dot_turned(wv_ref[...], normed).astype(BF)
    for pair in range(PAIRS):
        k_ref[pair] = keys[:, pair * 128 : (pair + 1) * 128]
        vt_ref[pair] = values[pair * 128 : (pair + 1) * 128]


def stale_call(pieces, gains, wk, wv):
    count, size = len(pieces), pieces[0].shape[0]
    patches, steps = size, 1
    cells = count * size * CELLS

    def piece_spec(i):
        def place(b, piece, step):
            return jnp.where(piece == i, step, jnp.where(piece < i, 0, steps - 1)), b, 0, 0

        return pl.BlockSpec((patches, None, CELLS, C), place)

    return pl.pallas_call(
        functools.partial(stale_kernel, count),
        grid=(2, count, steps),
        out_shape=[
            jax.ShapeDtypeStruct((2, PAIRS, cells, 128), BF),
            jax.ShapeDtypeStruct((2, PAIRS, 128, cells), BF),
        ],
        in_specs=[piece_spec(i) for i in range(count)]
        + [
            pl.BlockSpec((2, C), lambda b, piece, step: (0, 0)),
            pl.BlockSpec((None, C, C), lambda b, piece, step: (b, 0, 0)),
            pl.BlockSpec((None, C, C), lambda b, piece, step: (b, 0, 0)),
        ],
        out_specs=[
            pl.BlockSpec(
                (None, PAIRS, patches * CELLS, 128),
                lambda b, piece, step: (b, 0, piece * steps + step, 0),
            ),
            pl.BlockSpec(
                (None, PAIRS, 128, patches * CELLS),
                lambda b, piece, step: (b, 0, 0, piece * steps + step),
            ),
        ],
        compiler_params=pltpu.CompilerParams(vmem_limit_bytes=50 << 20),
        cost_estimate=pl.CostEstimate(
            flops=8 * cells * C * C, transcendentals=0, bytes_accessed=12 * cells * C
        ),
        name="stale_%d" % (count * size),
    )(*pieces, gains, wk, wv)


STORES = 3
NAMES = ("query", "key", "value", "out", "conv")


def block_kernel(*refs):
    x_ref, ga_ref, gc_ref, up_ref, dn_ref = refs[:5]
    own = dict(zip(NAMES, refs[5:10]))
    other = dict(zip(NAMES, refs[10:15]))
    k_hbm, v_hbm = refs[15 : 15 + STORES], refs[15 + STORES : 15 + 2 * STORES]
    o_ref, wqk, wv, wout, wconv, keys, values = refs[15 + 2 * STORES : 22 + 2 * STORES]
    queries, fresh, fresh_t, context, mid, cols, sem_w, sem_k = refs[22 + 2 * STORES :]
    core = lax.axis_index("segment") % 2
    targets = {
        "query": wqk.at[:, pl.ds(0, C)],
        "key": wqk.at[:, pl.ds(C, C)],
        "value": wv,
        "out": wout,
        "conv": wconv,
    }

    def start(place, *names):
        for name in names:
            start_copy(
                core == place,
                own[name],
                other[name],
                targets[name],
                sem_w.at[NAMES.index(name)],
            )

    def wait(name):
        wait_copy(own[name], targets[name], sem_w.at[NAMES.index(name)])

    def pair_copies(place, pair):
        copies, begin = [], 0
        for i in range(STORES):
            size = k_hbm[i].shape[2]
            cells = pl.ds(begin, size)
            begin += size
            for source, target, j in (
                (k_hbm[i].at[place, pair], keys.at[pair, cells, :], i),
                (v_hbm[i].at[place, pair], values.at[pair, :, cells], STORES + i),
            ):
                copies.append(pltpu.make_async_copy(source, target, sem_k.at[pair, j]))
        return copies

    start(0, "query", "key", "value")
    mid[...] = x_ref[...].astype(F32)
    lane = lax.broadcasted_iota(jnp.int32, (CELLS, 128), 1)
    own_cells = pl.ds(0, CELLS)

    def one_block(place, _):
        def ahead(work):
            pl.when(place == 0)(work)

        normed = normalize(mid[...], ga_ref[pl.ds(place, 1), :]).astype(BF)
        for name in NAMES[:3]:
            wait(name)

        @pl.when(place == 0)
        def _():
            for pair in range(PAIRS):
                for copy in pair_copies(0, pair):
                    copy.start()
            start(0, "out", "conv")

        made = dot(normed, wqk[...])
        turned_values = dot_turned(wv[...], normed).astype(BF)
        for pair in range(PAIRS):
            lanes = slice(pair * 128, (pair + 1) * 128)
            queries[pair] = (made[:, lanes] * QSCALE).astype(BF)
            fresh[pair] = made[:, C + pair * 128 : C + (pair + 1) * 128].astype(BF)
            fresh_t[pair] = turned_values[lanes]
        ahead(lambda: start(1, "query", "key", "value"))

        def attend(pair):
            for copy in pair_copies(0, pair):
                copy.wait()
            keys[pair, own_cells, :] = fresh[pair]
            values[pair, :, own_cells] = fresh_t[pair]
            both = queries[pair]
            zero = jnp.zeros_like(both)
            heads = jnp.concatenate(
                [jnp.where(lane < 64, both, zero), jnp.where(lane < 64, zero, both)], 0
            )
            totals = jnp.zeros((8, 2 * CELLS), F32)
            sums = [jnp.zeros((64, CELLS), F32)] * 2
            for chunk in range(KEYS // CHUNK):
                cells = pl.ds(chunk * CHUNK, CHUNK)
                weights = jnp.exp2(dot_t(keys[pair, cells, :], heads))
                totals = totals + jnp.sum(weights.reshape(CHUNK // 8, 8, 2 * CELLS), 0)
                weights = weights.astype(BF)
                for head in range(2):
                    sums[head] = sums[head] + dot(
                        values[pair, head * 64 : (head + 1) * 64, cells],
                        weights[:, head * CELLS : (head + 1) * CELLS],
                    )
            totals = jnp.sum(totals, axis=0, keepdims=True)
            ready = [sums[i] / totals[:, i * CELLS : (i + 1) * CELLS] for i in range(2)]
            context[pair] = jnp.concatenate(ready, 0).T.astype(BF)

            def next_pair():
                for copy in pair_copies(1, pair):
                    copy.start()

            ahead(next_pair)

        for pair in range(PAIRS):
            attend(pair)

        wait("out")
        x_mid = mid[...] + dot(
            jnp.concatenate([context[pair] for pair in range(PAIRS)], 1), wout[...]
        )
        mid[...] = x_mid
        ahead(lambda: start(1, "out"))
        gated = normalize(x_mid, gc_ref[pl.ds(place, 1), :])
        gated = gated / (1.0 + jnp.exp(-gated))
        gated = gated.astype(BF).astype(F32)
        rows = CELLS + 2 * W
        extended = jnp.concatenate(
            [up_ref[place].astype(F32), gated, dn_ref[place].astype(F32)], 0
        )
        col = lax.broadcasted_iota(jnp.int32, (rows, C), 0) % W
        cols[0] = jnp.where(col == 0, 0.0, pltpu.roll(extended, 1, 0)).astype(BF)
        cols[1] = extended.astype(BF)
        cols[2] = jnp.where(col == W - 1, 0.0, pltpu.roll(extended, rows - 1, 0)).astype(BF)
        wait("conv")

        def tap_row(i, _):
            cells = pl.ds(pl.multiple_of(i * W, W), CELLS)
            total = mid[...]
            for j in range(3):
                total = total + dot(cols[j, cells, :], wconv[3 * i + j])
            mid[...] = total
            return 0

        lax.fori_loop(0, 3, tap_row, 0)
        ahead(lambda: start(1, "conv"))
        return 0

    lax.fori_loop(0, 2, one_block, 0)
    o_ref[...] = mid[...].astype(o_ref.dtype)


def block_call(x, gain_attn, gain_conv, up, down, own, other, stored):
    vmem = pl.BlockSpec(memory_space=pltpu.VMEM)
    hbm = pl.BlockSpec(memory_space=pltpu.HBM)
    return pl.pallas_call(
        block_kernel,
        out_shape=jax.ShapeDtypeStruct((CELLS, C), BF),
        in_specs=[vmem] * 5 + [hbm] * (10 + 2 * STORES),
        out_specs=vmem,
        scratch_shapes=[
            pltpu.VMEM((C, 2 * C), BF),
            pltpu.VMEM((C, C), BF),
            pltpu.VMEM((C, C), BF),
            pltpu.VMEM((9, C, C), BF),
            pltpu.VMEM((PAIRS, KEYS, 128), BF),
            pltpu.VMEM((PAIRS, 128, KEYS), BF),
            pltpu.VMEM((PAIRS, CELLS, 128), BF),
            pltpu.VMEM((PAIRS, CELLS, 128), BF),
            pltpu.VMEM((PAIRS, 128, CELLS), BF),
            pltpu.VMEM((PAIRS, CELLS, 128), BF),
            pltpu.VMEM((CELLS, C), F32),
            pltpu.VMEM((3, CELLS + 2 * W, C), BF),
            pltpu.SemaphoreType.DMA((5,)),
            pltpu.SemaphoreType.DMA((PAIRS, 2 * STORES)),
        ],
        compiler_params=pltpu.CompilerParams(vmem_limit_bytes=58 << 20),
        cost_estimate=pl.CostEstimate(
            flops=2 * 13_000_000_000,
            transcendentals=2 * 10_500_000,
            bytes_accessed=2 * 22_000_000,
        ),
        name="blocks",
    )(
        x,
        gain_attn,
        gain_conv,
        up,
        down,
        *[own[name] for name in NAMES],
        *[other[name] for name in NAMES],
        *[pair[0] for pair in stored],
        *[pair[1] for pair in stored],
    )


def turned(value, leg, by):
    pairs = []
    for segment in range(8):
        for y in range(4):
            for z in range(4):
                if segment % 2 == leg:
                    to = y, (z + by) % 4
                else:
                    to = (y + by) % 4, z
                pairs.append((16 * segment + 4 * y + z, 16 * segment + 4 * to[0] + to[1]))
    return lax.ppermute(value, ("segment", "patch"), pairs)


def ring_near(value, leg):
    return turned(value, leg, 1), turned(value, leg, -1)


def ring_far(back, ahead, leg):
    half = back.shape[0] // 2
    return turned(back[:half], leg, 1), turned(ahead[half:], leg, -1)


def shards(
    latent, stale_attn, stale_edge, norm_attn, query_w, key_w, value_w, out_w, norm_conv, conv_w
):
    core = lax.axis_index("segment") % 2
    is_first = core == 0
    sibling = [(i, i ^ 1) for i in range(8)]

    def swap(value):
        return lax.ppermute(value, "segment", sibling)

    def ordered(own, other):
        return jnp.where(is_first, own, other), jnp.where(is_first, other, own)

    def exchanged(value):
        keep = lax.dynamic_index_in_dim(value, core, 0, keepdims=False)
        give = lax.dynamic_index_in_dim(value, 1 - core, 0, keepdims=False)
        return ordered(keep, swap(give))

    own = dict(zip(NAMES, (query_w[0], key_w[0], value_w[0], out_w[0], conv_w[0].reshape(9, C, C))))
    mine = jnp.concatenate(
        [stale_attn[0].reshape(2, CELLS, C), stale_edge[0].reshape(2, 2 * W, C)], 1
    )
    mine = jnp.stack(exchanged(mine))
    raw, edges = mine[:, :CELLS], mine[:, CELLS:].reshape(2, 2, W, C)
    raw, first_sent, norm_attn = lax.optimization_barrier(
        (raw, {name: own[name] for name in ("key", "value")}, norm_attn)
    )
    other = {name: swap(value) for name, value in first_sent.items()}
    gains = jnp.concatenate(ordered(norm_attn, swap(norm_attn)), 0)
    wk, wv = [jnp.stack(ordered(own[name], other[name])) for name in ("key", "value")]
    back, ahead = ring_near(raw, 0)
    own_back, own_ahead = ring_near(raw, 1)
    far = ring_far(back, ahead, 0)
    rest = jnp.stack([back, jnp.concatenate(far, 0), ahead])
    first = jnp.stack([raw, own_back, own_ahead])
    rest, first, sent, edges, norm_conv = lax.optimization_barrier(
        (rest, first, {name: own[name] for name in ("query", "out", "conv")}, edges, norm_conv)
    )
    back, ahead = ring_near(rest, 1)
    upper = lax.ppermute(edges[:, 1], "patch", [(i, i + 1) for i in range(15)])
    lower = lax.ppermute(edges[:, 0], "patch", [(i + 1, i) for i in range(15)])
    stored = stale_call([first, rest], gains, wk, wv)
    back, ahead, upper, lower, stored = lax.optimization_barrier(
        (back, ahead, upper, lower, stored)
    )
    far = (
        turned(jnp.concatenate([first[1:2], back[:1]], 0), 1, 1),
        turned(ahead[1:], 1, -1),
    )

    other |= {name: swap(value) for name, value in sent.items()}
    conv_gains = jnp.concatenate(ordered(norm_conv, swap(norm_conv)), 0)

    x = lax.dynamic_index_in_dim(latent, core, 0, keepdims=False).reshape(CELLS, C)
    stored = [stored] + [stale_call(pieces, gains, wk, wv) for pieces in ([back, ahead], far)]

    def two_blocks(x):
        return block_call(x, gains, conv_gains, upper, lower, own, other, stored)

    def hop(x):
        return lax.ppermute(x, "segment", [(i, i + 2) for i in range(6)])

    def chip_stage(stage, x):
        return lax.cond(stage < 3, hop, lambda x: x, two_blocks(x))

    x = lax.fori_loop(0, 4, chip_stage, x)

    groups = x.reshape(4, 4, 2, 8, C)
    keep = lax.dynamic_index_in_dim(groups, core, 2, keepdims=False)
    got = swap(lax.dynamic_index_in_dim(groups, 1 - core, 2, keepdims=False))
    both = jnp.stack(ordered(keep, got))
    result = jnp.where(lax.axis_index("segment") >= 6, both[:, :, 3], jnp.zeros_like(both[:, :, 3]))
    for d in (1, 2, 3):
        result = result + lax.ppermute(
            both[:, :, (3 + d) % 4], "segment", [(6, (6 + 2 * d) % 8), (7, (7 + 2 * d) % 8)]
        )
    return result.astype(F32)


def solution(mesh):
    in_specs = (
        P(None, "patch", None, None),
        P("segment", None, "patch", None, None),
        P("segment", None, "patch", None, None),
        P("segment", None),
        P("segment", None, None),
        P("segment", None, None),
        P("segment", None, None),
        P("segment", None, None),
        P("segment", None),
        P("segment", None, None, None, None),
    )
    out_specs = P(None, "patch", "segment", None)
    return jax.shard_map(shards, mesh=mesh, in_specs=in_specs, out_specs=out_specs, check_vma=False)
```

```python
import functools

import jax
import jax.numpy as jnp
from jax import lax
from jax.experimental import pallas as pl
from jax.experimental.pallas import tpu as pltpu
from jax.sharding import PartitionSpec as P

C = 640
PAIRS = 5
CELLS = 256
W = 64
KEYS = 4096
CHUNK = 2048
F32 = jnp.float32
BF = jnp.bfloat16
QSCALE = 0.125 * 1.4426950408889634


def normalize(values, gain):
    center = values - jnp.mean(values, axis=-1, keepdims=True)
    spread = jnp.mean(center * center, axis=-1, keepdims=True)
    return center * lax.rsqrt(spread + 1e-05) * gain


def dot(a, b):
    return jnp.dot(a, b, preferred_element_type=F32)


def dot_t(a, b):
    return lax.dot_general(a, b, (((1,), (1,)), ((), ())), preferred_element_type=F32)


def dot_turned(a, b):
    return lax.dot_general(a, b, (((0,), (1,)), ((), ())), preferred_element_type=F32)


def start_copy(use_own, own, other, target, sem):
    @pl.when(use_own)
    def _():
        pltpu.make_async_copy(own, target, sem).start()

    @pl.when(jnp.logical_not(use_own))
    def _():
        pltpu.make_async_copy(other, target, sem).start()


def wait_copy(own, target, sem):
    pltpu.make_async_copy(own, target, sem).wait()


def stale_kernel(count, *refs):
    pieces, (ga_ref, wk_ref, wv_ref, k_ref, vt_ref) = refs[:count], refs[count:]
    block, piece = pl.program_id(0), pl.program_id(1)
    raw = pieces[0][...]
    for i in range(1, count):
        raw = jnp.where(piece == i, pieces[i][...], raw)
    raw = raw.reshape(-1, C).astype(F32)
    normed = normalize(raw, ga_ref[pl.ds(block, 1), :]).astype(BF)
    keys = dot(normed, wk_ref[...]).astype(BF)
    values = dot_turned(wv_ref[...], normed).astype(BF)
    for pair in range(PAIRS):
        k_ref[pair] = keys[:, pair * 128 : (pair + 1) * 128]
        vt_ref[pair] = values[pair * 128 : (pair + 1) * 128]


def stale_call(pieces, gains, wk, wv):
    count, size = len(pieces), pieces[0].shape[0]
    patches, steps = size, 1
    cells = count * size * CELLS

    def piece_spec(i):
        def place(b, piece, step):
            return jnp.where(piece == i, step, jnp.where(piece < i, 0, steps - 1)), b, 0, 0

        return pl.BlockSpec((patches, None, CELLS, C), place)

    return pl.pallas_call(
        functools.partial(stale_kernel, count),
        grid=(2, count, steps),
        out_shape=[
            jax.ShapeDtypeStruct((2, PAIRS, cells, 128), BF),
            jax.ShapeDtypeStruct((2, PAIRS, 128, cells), BF),
        ],
        in_specs=[piece_spec(i) for i in range(count)]
        + [
            pl.BlockSpec((2, C), lambda b, piece, step: (0, 0)),
            pl.BlockSpec((None, C, C), lambda b, piece, step: (b, 0, 0)),
            pl.BlockSpec((None, C, C), lambda b, piece, step: (b, 0, 0)),
        ],
        out_specs=[
            pl.BlockSpec(
                (None, PAIRS, patches * CELLS, 128),
                lambda b, piece, step: (b, 0, piece * steps + step, 0),
            ),
            pl.BlockSpec(
                (None, PAIRS, 128, patches * CELLS),
                lambda b, piece, step: (b, 0, 0, piece * steps + step),
            ),
        ],
        compiler_params=pltpu.CompilerParams(vmem_limit_bytes=50 << 20),
        cost_estimate=pl.CostEstimate(
            flops=8 * cells * C * C, transcendentals=0, bytes_accessed=12 * cells * C
        ),
        name="stale",
    )(*pieces, gains, wk, wv)


STORES = 4
NAMES = ("query", "key", "value", "out", "conv")


def block_kernel(*refs):
    x_ref, ga_ref, gc_ref, up_ref, dn_ref = refs[:5]
    own = dict(zip(NAMES, refs[5:10]))
    other = dict(zip(NAMES, refs[10:15]))
    k_hbm, v_hbm = refs[15 : 15 + STORES], refs[15 + STORES : 15 + 2 * STORES]
    o_ref, wqk, wv, wout, wconv, keys, values = refs[15 + 2 * STORES : 22 + 2 * STORES]
    queries, fresh, fresh_t, context, mid, cols, sem_w, sem_k = refs[22 + 2 * STORES :]
    core = lax.axis_index("segment") % 2
    targets = {
        "query": wqk.at[:, pl.ds(0, C)],
        "key": wqk.at[:, pl.ds(C, C)],
        "value": wv,
        "out": wout,
        "conv": wconv,
    }

    def start(place, *names):
        for name in names:
            start_copy(
                core == place,
                own[name],
                other[name],
                targets[name],
                sem_w.at[NAMES.index(name)],
            )

    def wait(name):
        wait_copy(own[name], targets[name], sem_w.at[NAMES.index(name)])

    def pair_copies(place, pair):
        copies, begin = [], 0
        for i in range(STORES):
            size = k_hbm[i].shape[2]
            cells = pl.ds(begin, size)
            begin += size
            for source, target, j in (
                (k_hbm[i].at[place, pair], keys.at[pair, cells, :], i),
                (v_hbm[i].at[place, pair], values.at[pair, :, cells], STORES + i),
            ):
                copies.append(pltpu.make_async_copy(source, target, sem_k.at[pair, j]))
        return copies

    start(0, "query", "key", "value")
    mid[...] = x_ref[...].astype(F32)
    lane = lax.broadcasted_iota(jnp.int32, (CELLS, 128), 1)
    own_cells = pl.ds(0, CELLS)

    def one_block(place, _):
        def ahead(work):
            pl.when(place == 0)(work)

        normed = normalize(mid[...], ga_ref[pl.ds(place, 1), :]).astype(BF)
        for name in NAMES[:3]:
            wait(name)

        @pl.when(place == 0)
        def _():
            for pair in range(PAIRS):
                for copy in pair_copies(0, pair):
                    copy.start()
            start(0, "out", "conv")

        made = dot(normed, wqk[...])
        turned_values = dot_turned(wv[...], normed).astype(BF)
        for pair in range(PAIRS):
            lanes = slice(pair * 128, (pair + 1) * 128)
            queries[pair] = (made[:, lanes] * QSCALE).astype(BF)
            fresh[pair] = made[:, C + pair * 128 : C + (pair + 1) * 128].astype(BF)
            fresh_t[pair] = turned_values[lanes]
        ahead(lambda: start(1, "query", "key", "value"))

        def attend(pair):
            for copy in pair_copies(0, pair):
                copy.wait()
            keys[pair, own_cells, :] = fresh[pair]
            values[pair, :, own_cells] = fresh_t[pair]
            both = queries[pair]
            zero = jnp.zeros_like(both)
            heads = jnp.concatenate(
                [jnp.where(lane < 64, both, zero), jnp.where(lane < 64, zero, both)], 0
            )
            totals = jnp.zeros((8, 2 * CELLS), F32)
            sums = [jnp.zeros((64, CELLS), F32)] * 2
            for chunk in range(KEYS // CHUNK):
                cells = pl.ds(chunk * CHUNK, CHUNK)
                weights = jnp.exp2(dot_t(keys[pair, cells, :], heads))
                totals = totals + jnp.sum(weights.reshape(CHUNK // 8, 8, 2 * CELLS), 0)
                weights = weights.astype(BF)
                for head in range(2):
                    sums[head] = sums[head] + dot(
                        values[pair, head * 64 : (head + 1) * 64, cells],
                        weights[:, head * CELLS : (head + 1) * CELLS],
                    )
            totals = jnp.sum(totals, axis=0, keepdims=True)
            ready = [sums[i] / totals[:, i * CELLS : (i + 1) * CELLS] for i in range(2)]
            context[pair] = jnp.concatenate(ready, 0).T.astype(BF)

            def next_pair():
                for copy in pair_copies(1, pair):
                    copy.start()

            ahead(next_pair)

        for pair in range(PAIRS):
            attend(pair)

        wait("out")
        x_mid = mid[...] + dot(
            jnp.concatenate([context[pair] for pair in range(PAIRS)], 1), wout[...]
        )
        mid[...] = x_mid
        ahead(lambda: start(1, "out"))
        gated = normalize(x_mid, gc_ref[pl.ds(place, 1), :])
        gated = gated / (1.0 + jnp.exp(-gated))
        gated = gated.astype(BF).astype(F32)
        rows = CELLS + 2 * W
        extended = jnp.concatenate(
            [up_ref[place].astype(F32), gated, dn_ref[place].astype(F32)], 0
        )
        col = lax.broadcasted_iota(jnp.int32, (rows, C), 0) % W
        cols[0] = jnp.where(col == 0, 0.0, pltpu.roll(extended, 1, 0)).astype(BF)
        cols[1] = extended.astype(BF)
        cols[2] = jnp.where(col == W - 1, 0.0, pltpu.roll(extended, rows - 1, 0)).astype(BF)
        wait("conv")

        def tap_row(i, _):
            cells = pl.ds(pl.multiple_of(i * W, W), CELLS)
            total = mid[...]
            for j in range(3):
                total = total + dot(cols[j, cells, :], wconv[3 * i + j])
            mid[...] = total
            return 0

        lax.fori_loop(0, 3, tap_row, 0)
        ahead(lambda: start(1, "conv"))
        return 0

    lax.fori_loop(0, 2, one_block, 0)
    o_ref[...] = mid[...].astype(o_ref.dtype)


def block_call(x, gain_attn, gain_conv, up, down, own, other, stored):
    vmem = pl.BlockSpec(memory_space=pltpu.VMEM)
    hbm = pl.BlockSpec(memory_space=pltpu.HBM)
    return pl.pallas_call(
        block_kernel,
        out_shape=jax.ShapeDtypeStruct((CELLS, C), BF),
        in_specs=[vmem] * 5 + [hbm] * (10 + 2 * STORES),
        out_specs=vmem,
        scratch_shapes=[
            pltpu.VMEM((C, 2 * C), BF),
            pltpu.VMEM((C, C), BF),
            pltpu.VMEM((C, C), BF),
            pltpu.VMEM((9, C, C), BF),
            pltpu.VMEM((PAIRS, KEYS, 128), BF),
            pltpu.VMEM((PAIRS, 128, KEYS), BF),
            pltpu.VMEM((PAIRS, CELLS, 128), BF),
            pltpu.VMEM((PAIRS, CELLS, 128), BF),
            pltpu.VMEM((PAIRS, 128, CELLS), BF),
            pltpu.VMEM((PAIRS, CELLS, 128), BF),
            pltpu.VMEM((CELLS, C), F32),
            pltpu.VMEM((3, CELLS + 2 * W, C), BF),
            pltpu.SemaphoreType.DMA((5,)),
            pltpu.SemaphoreType.DMA((PAIRS, 2 * STORES)),
        ],
        compiler_params=pltpu.CompilerParams(vmem_limit_bytes=58 << 20),
        cost_estimate=pl.CostEstimate(
            flops=2 * 13_000_000_000,
            transcendentals=2 * 10_500_000,
            bytes_accessed=2 * 22_000_000,
        ),
        name="blocks",
    )(
        x,
        gain_attn,
        gain_conv,
        up,
        down,
        *[own[name] for name in NAMES],
        *[other[name] for name in NAMES],
        *[pair[0] for pair in stored],
        *[pair[1] for pair in stored],
    )


def turned(value, leg, by):
    pairs = []
    for segment in range(8):
        for y in range(4):
            for z in range(4):
                if segment % 2 == leg:
                    to = y, (z + by) % 4
                else:
                    to = (y + by) % 4, z
                pairs.append((16 * segment + 4 * y + z, 16 * segment + 4 * to[0] + to[1]))
    return lax.ppermute(value, ("segment", "patch"), pairs)


def ring_near(value, leg):
    return turned(value, leg, 1), turned(value, leg, -1)


def ring_far(back, ahead, leg):
    half = back.shape[0] // 2
    return turned(back[:half], leg, 1), turned(ahead[half:], leg, -1)


def shards(
    latent, stale_attn, stale_edge, norm_attn, query_w, key_w, value_w, out_w, norm_conv, conv_w
):
    core = lax.axis_index("segment") % 2
    is_first = core == 0
    sibling = [(i, i ^ 1) for i in range(8)]

    def swap(value):
        return lax.ppermute(value, "segment", sibling)

    def ordered(own, other):
        return jnp.where(is_first, own, other), jnp.where(is_first, other, own)

    def exchanged(value):
        keep = lax.dynamic_index_in_dim(value, core, 0, keepdims=False)
        give = lax.dynamic_index_in_dim(value, 1 - core, 0, keepdims=False)
        return ordered(keep, swap(give))

    own = dict(zip(NAMES, (query_w[0], key_w[0], value_w[0], out_w[0], conv_w[0].reshape(9, C, C))))
    mine = jnp.concatenate(
        [stale_attn[0].reshape(2, CELLS, C), stale_edge[0].reshape(2, 2 * W, C)], 1
    )
    mine = jnp.stack(exchanged(mine))
    raw, edges = mine[:, :CELLS], mine[:, CELLS:].reshape(2, 2, W, C)
    gains = jnp.concatenate(ordered(norm_attn, swap(norm_attn)), 0)
    conv_gains = jnp.concatenate(ordered(norm_conv, swap(norm_conv)), 0)
    raw, sent = lax.optimization_barrier(
        (raw, {name: own[name] for name in ("key", "value")})
    )
    other = {name: swap(value) for name, value in sent.items()}
    wk, wv = [jnp.stack(ordered(own[name], other[name])) for name in ("key", "value")]
    back, ahead = ring_near(raw, 0)
    far = ring_far(back, ahead, 0)
    back, ahead, far, wk, wv, gains, edges, conv_sent = lax.optimization_barrier(
        (back, ahead, far, wk, wv, gains, edges, own["conv"])
    )
    other["conv"] = swap(conv_sent)
    row = jnp.stack([raw, back]), jnp.stack([jnp.concatenate(far, 0), ahead])
    first = turned(row[0], 1, 1), turned(row[1], 1, -1)
    second = turned(row[1], 1, 1), turned(row[0], 1, -1)
    upper = lax.ppermute(edges[:, 1], "patch", [(i, i + 1) for i in range(15)])
    lower = lax.ppermute(edges[:, 0], "patch", [(i + 1, i) for i in range(15)])
    stored = [stale_call(row, gains, wk, wv)]
    first, upper, lower, stored = lax.optimization_barrier((first, upper, lower, stored))
    far = turned(first[0], 1, 1), turned(first[1], 1, -1)
    stored.append(stale_call(first, gains, wk, wv))
    second, stored, sent = lax.optimization_barrier(
        (second, stored, {name: own[name] for name in ("query", "out")})
    )
    other |= {name: swap(value) for name, value in sent.items()}
    stored += [stale_call(pieces, gains, wk, wv) for pieces in (second, far)]

    x = lax.dynamic_index_in_dim(latent, core, 0, keepdims=False).reshape(CELLS, C)
    def two_blocks(x):
        return block_call(x, gains, conv_gains, upper, lower, own, other, stored)

    def hop(x):
        return lax.ppermute(x, "segment", [(i, i + 2) for i in range(6)])

    def chip_stage(stage, x):
        return lax.cond(stage < 3, hop, lambda x: x, two_blocks(x))

    x = lax.fori_loop(0, 4, chip_stage, x)

    groups = x.reshape(4, 4, 2, 8, C)
    keep = lax.dynamic_index_in_dim(groups, core, 2, keepdims=False)
    got = swap(lax.dynamic_index_in_dim(groups, 1 - core, 2, keepdims=False))
    both = jnp.stack(ordered(keep, got))
    result = jnp.where(lax.axis_index("segment") >= 6, both[:, :, 3], jnp.zeros_like(both[:, :, 3]))
    for d in (1, 2, 3):
        result = result + lax.ppermute(
            both[:, :, (3 + d) % 4], "segment", [(6, (6 + 2 * d) % 8), (7, (7 + 2 * d) % 8)]
        )
    return result.astype(F32)


def solution(mesh):
    in_specs = (
        P(None, "patch", None, None),
        P("segment", None, "patch", None, None),
        P("segment", None, "patch", None, None),
        P("segment", None),
        P("segment", None, None),
        P("segment", None, None),
        P("segment", None, None),
        P("segment", None, None),
        P("segment", None),
        P("segment", None, None, None, None),
    )
    out_specs = P(None, "patch", "segment", None)
    return jax.shard_map(shards, mesh=mesh, in_specs=in_specs, out_specs=out_specs, check_vma=False)
```

```python
import functools

import jax
import jax.numpy as jnp
from jax import lax
from jax.experimental import pallas as pl
from jax.experimental.pallas import tpu as pltpu
from jax.sharding import PartitionSpec as P

C = 640
PAIRS = 5
CELLS = 256
W = 64
KEYS = 4096
CHUNK = 2048
F32 = jnp.float32
BF = jnp.bfloat16
QSCALE = 0.125 * 1.4426950408889634


def normalize(values, gain):
    center = values - jnp.mean(values, axis=-1, keepdims=True)
    spread = jnp.mean(center * center, axis=-1, keepdims=True)
    return center * lax.rsqrt(spread + 1e-05) * gain


def dot(a, b):
    return jnp.dot(a, b, preferred_element_type=F32)


def dot_t(a, b):
    return lax.dot_general(a, b, (((1,), (1,)), ((), ())), preferred_element_type=F32)


def dot_turned(a, b):
    return lax.dot_general(a, b, (((0,), (1,)), ((), ())), preferred_element_type=F32)


def start_copy(use_own, own, other, target, sem):
    @pl.when(use_own)
    def _():
        pltpu.make_async_copy(own, target, sem).start()

    @pl.when(jnp.logical_not(use_own))
    def _():
        pltpu.make_async_copy(other, target, sem).start()


def wait_copy(own, target, sem):
    pltpu.make_async_copy(own, target, sem).wait()


def stale_kernel(near_ref, far_ref, ga_ref, wk_ref, wv_ref, k_ref, vt_ref):
    block = pl.program_id(0)
    raw = jnp.concatenate([near_ref[...], far_ref[...]], 0).reshape(-1, C).astype(F32)
    normed = normalize(raw, ga_ref[pl.ds(block, 1), :]).astype(BF)
    keys = dot(normed, wk_ref[...]).astype(BF)
    for pair in range(PAIRS):
        k_ref[pair] = keys[:, pair * 128 : (pair + 1) * 128]
    values = dot_turned(wv_ref[...], normed).astype(BF)
    for pair in range(PAIRS):
        vt_ref[pair] = values[pair * 128 : (pair + 1) * 128]


def stale_call(pieces, gains, wk, wv):
    size = pieces[0].shape[0]
    cells = 2 * size * CELLS
    return pl.pallas_call(
        stale_kernel,
        grid=(2,),
        out_shape=[
            jax.ShapeDtypeStruct((2, PAIRS, cells, 128), BF),
            jax.ShapeDtypeStruct((2, PAIRS, 128, cells), BF),
        ],
        in_specs=[
            pl.BlockSpec((size, None, CELLS, C), lambda b: (0, b, 0, 0)),
            pl.BlockSpec((size, None, CELLS, C), lambda b: (0, b, 0, 0)),
            pl.BlockSpec((2, C), lambda b: (0, 0)),
            pl.BlockSpec((None, C, C), lambda b: (b, 0, 0)),
            pl.BlockSpec((None, C, C), lambda b: (b, 0, 0)),
        ],
        out_specs=[
            pl.BlockSpec((None, PAIRS, cells, 128), lambda b: (b, 0, 0, 0)),
            pl.BlockSpec((None, PAIRS, 128, cells), lambda b: (b, 0, 0, 0)),
        ],
        compiler_params=pltpu.CompilerParams(vmem_limit_bytes=50 << 20),
        cost_estimate=pl.CostEstimate(
            flops=8 * cells * C * C, transcendentals=0, bytes_accessed=12 * cells * C
        ),
        name="stale",
    )(*pieces, gains, wk, wv)


STORES = 4
NAMES = ("query", "key", "value", "out", "conv")


def block_kernel(*refs):
    x_ref, ga_ref, gc_ref, up_ref, dn_ref = refs[:5]
    own = dict(zip(NAMES, refs[5:10]))
    other = dict(zip(NAMES, refs[10:15]))
    k_hbm, v_hbm = refs[15 : 15 + STORES], refs[15 + STORES : 15 + 2 * STORES]
    o_ref, wqk, wv, wout, wconv, keys, values = refs[15 + 2 * STORES : 22 + 2 * STORES]
    queries, fresh, fresh_t, context, mid, cols, sem_w, sem_k = refs[22 + 2 * STORES :]
    core = lax.axis_index("segment") % 2
    targets = {
        "query": wqk.at[:, pl.ds(0, C)],
        "key": wqk.at[:, pl.ds(C, C)],
        "value": wv,
        "out": wout,
        "conv": wconv,
    }

    def start(place, *names):
        for name in names:
            start_copy(
                core == place,
                own[name],
                other[name],
                targets[name],
                sem_w.at[NAMES.index(name)],
            )

    def wait(name):
        wait_copy(own[name], targets[name], sem_w.at[NAMES.index(name)])

    def pair_copies(place, pair):
        copies, begin = [], 0
        for i in range(STORES):
            size = k_hbm[i].shape[2]
            cells = pl.ds(begin, size)
            begin += size
            for source, target, j in (
                (k_hbm[i].at[place, pair], keys.at[pair, cells, :], i),
                (v_hbm[i].at[place, pair], values.at[pair, :, cells], STORES + i),
            ):
                copies.append(pltpu.make_async_copy(source, target, sem_k.at[pair, j]))
        return copies

    start(0, "query", "key", "value")
    for copy in pair_copies(0, 0):
        copy.start()
    mid[...] = x_ref[...].astype(F32)
    lane = lax.broadcasted_iota(jnp.int32, (CELLS, 128), 1)
    own_cells = pl.ds(0, CELLS)

    def one_block(place, _):
        def ahead(work):
            pl.when(place == 0)(work)

        normed = normalize(mid[...], ga_ref[pl.ds(place, 1), :]).astype(BF)
        for name in NAMES[:3]:
            wait(name)

        @pl.when(place == 0)
        def _():
            for pair in range(1, PAIRS):
                for copy in pair_copies(0, pair):
                    copy.start()
            start(0, "out", "conv")

        made = dot(normed, wqk[...])
        turned_values = dot_turned(wv[...], normed).astype(BF)
        for pair in range(PAIRS):
            lanes = slice(pair * 128, (pair + 1) * 128)
            queries[pair] = (made[:, lanes] * QSCALE).astype(BF)
            fresh[pair] = made[:, C + pair * 128 : C + (pair + 1) * 128].astype(BF)
            fresh_t[pair] = turned_values[lanes]
        ahead(lambda: start(1, "query", "key", "value"))

        def attend(pair):
            for copy in pair_copies(0, pair):
                copy.wait()
            keys[pair, own_cells, :] = fresh[pair]
            values[pair, :, own_cells] = fresh_t[pair]
            both = queries[pair]
            zero = jnp.zeros_like(both)
            heads = jnp.concatenate(
                [jnp.where(lane < 64, both, zero), jnp.where(lane < 64, zero, both)], 0
            )
            totals = jnp.zeros((8, 2 * CELLS), F32)
            sums = [jnp.zeros((64, CELLS), F32)] * 2
            for chunk in range(KEYS // CHUNK):
                cells = pl.ds(chunk * CHUNK, CHUNK)
                weights = jnp.exp2(dot_t(keys[pair, cells, :], heads))
                totals = totals + jnp.sum(weights.reshape(CHUNK // 8, 8, 2 * CELLS), 0)
                weights = weights.astype(BF)
                for head in range(2):
                    sums[head] = sums[head] + dot(
                        values[pair, head * 64 : (head + 1) * 64, cells],
                        weights[:, head * CELLS : (head + 1) * CELLS],
                    )
            totals = jnp.sum(totals, axis=0, keepdims=True)
            ready = [sums[i] / totals[:, i * CELLS : (i + 1) * CELLS] for i in range(2)]
            context[pair] = jnp.concatenate(ready, 0).T.astype(BF)

            def next_pair():
                for copy in pair_copies(1, pair):
                    copy.start()

            ahead(next_pair)

        for pair in range(PAIRS):
            attend(pair)

        wait("out")
        x_mid = mid[...] + dot(
            jnp.concatenate([context[pair] for pair in range(PAIRS)], 1), wout[...]
        )
        mid[...] = x_mid
        ahead(lambda: start(1, "out"))
        gated = normalize(x_mid, gc_ref[pl.ds(place, 1), :])
        gated = gated / (1.0 + jnp.exp(-gated))
        gated = gated.astype(BF).astype(F32)
        rows = CELLS + 2 * W
        extended = jnp.concatenate(
            [up_ref[place].astype(F32), gated, dn_ref[place].astype(F32)], 0
        )
        col = lax.broadcasted_iota(jnp.int32, (rows, C), 0) % W
        cols[0] = jnp.where(col == 0, 0.0, pltpu.roll(extended, 1, 0)).astype(BF)
        cols[1] = extended.astype(BF)
        cols[2] = jnp.where(col == W - 1, 0.0, pltpu.roll(extended, rows - 1, 0)).astype(BF)
        wait("conv")

        def tap_row(i, _):
            cells = pl.ds(pl.multiple_of(i * W, W), CELLS)
            total = mid[...]
            for j in range(3):
                total = total + dot(cols[j, cells, :], wconv[3 * i + j])
            mid[...] = total
            return 0

        lax.fori_loop(0, 3, tap_row, 0)
        ahead(lambda: start(1, "conv"))
        return 0

    lax.fori_loop(0, 2, one_block, 0)
    o_ref[...] = mid[...].astype(o_ref.dtype)


def block_call(x, gain_attn, gain_conv, up, down, own, other, stored):
    vmem = pl.BlockSpec(memory_space=pltpu.VMEM)
    hbm = pl.BlockSpec(memory_space=pltpu.HBM)
    return pl.pallas_call(
        block_kernel,
        out_shape=jax.ShapeDtypeStruct((CELLS, C), BF),
        in_specs=[vmem] * 5 + [hbm] * (10 + 2 * STORES),
        out_specs=vmem,
        scratch_shapes=[
            pltpu.VMEM((C, 2 * C), BF),
            pltpu.VMEM((C, C), BF),
            pltpu.VMEM((C, C), BF),
            pltpu.VMEM((9, C, C), BF),
            pltpu.VMEM((PAIRS, KEYS, 128), BF),
            pltpu.VMEM((PAIRS, 128, KEYS), BF),
            pltpu.VMEM((PAIRS, CELLS, 128), BF),
            pltpu.VMEM((PAIRS, CELLS, 128), BF),
            pltpu.VMEM((PAIRS, 128, CELLS), BF),
            pltpu.VMEM((PAIRS, CELLS, 128), BF),
            pltpu.VMEM((CELLS, C), F32),
            pltpu.VMEM((3, CELLS + 2 * W, C), BF),
            pltpu.SemaphoreType.DMA((5,)),
            pltpu.SemaphoreType.DMA((PAIRS, 2 * STORES)),
        ],
        compiler_params=pltpu.CompilerParams(vmem_limit_bytes=58 << 20),
        cost_estimate=pl.CostEstimate(
            flops=2 * 13_000_000_000,
            transcendentals=2 * 10_500_000,
            bytes_accessed=2 * 22_000_000,
        ),
        name="blocks",
    )(
        x,
        gain_attn,
        gain_conv,
        up,
        down,
        *[own[name] for name in NAMES],
        *[other[name] for name in NAMES],
        *[pair[0] for pair in stored],
        *[pair[1] for pair in stored],
    )


def turned(value, leg, by):
    pairs = []
    for segment in range(8):
        for y in range(4):
            for z in range(4):
                if segment % 2 == leg:
                    to = y, (z + by) % 4
                else:
                    to = (y + by) % 4, z
                pairs.append((16 * segment + 4 * y + z, 16 * segment + 4 * to[0] + to[1]))
    return lax.ppermute(value, ("segment", "patch"), pairs)


def ring_near(value, leg):
    return turned(value, leg, 1), turned(value, leg, -1)


def ring_far(back, ahead, leg):
    half = back.shape[0] // 2
    return turned(back[:half], leg, 1), turned(ahead[half:], leg, -1)


def shards(
    latent, stale_attn, stale_edge, norm_attn, query_w, key_w, value_w, out_w, norm_conv, conv_w
):
    core = lax.axis_index("segment") % 2
    is_first = core == 0
    sibling = [(i, i ^ 1) for i in range(8)]

    def swap(value):
        return lax.ppermute(value, "segment", sibling)

    def ordered(own, other):
        return jnp.where(is_first, own, other), jnp.where(is_first, other, own)

    def exchanged(value):
        keep = lax.dynamic_index_in_dim(value, core, 0, keepdims=False)
        give = lax.dynamic_index_in_dim(value, 1 - core, 0, keepdims=False)
        return ordered(keep, swap(give))

    own = dict(zip(NAMES, (query_w[0], key_w[0], value_w[0], out_w[0], conv_w[0].reshape(9, C, C))))
    mine = jnp.concatenate(
        [stale_attn[0].reshape(2, CELLS, C), stale_edge[0].reshape(2, 2 * W, C)], 1
    )
    mine = jnp.stack(exchanged(mine))
    raw, edges = mine[:, :CELLS], mine[:, CELLS:].reshape(2, 2, W, C)
    gains = jnp.concatenate(ordered(norm_attn, swap(norm_attn)), 0)
    conv_gains = jnp.concatenate(ordered(norm_conv, swap(norm_conv)), 0)
    raw, sent = lax.optimization_barrier(
        (raw, {name: own[name] for name in ("key", "value")})
    )
    other = {name: swap(value) for name, value in sent.items()}
    wk, wv = [jnp.stack(ordered(own[name], other[name])) for name in ("key", "value")]
    back, ahead = ring_near(raw, 0)
    far = ring_far(back, ahead, 0)
    upper = lax.ppermute(edges[:, 1], "patch", [(i, i + 1) for i in range(15)])
    lower = lax.ppermute(edges[:, 0], "patch", [(i + 1, i) for i in range(15)])
    back, ahead, far, wk, wv, gains, upper, lower, conv_sent = lax.optimization_barrier(
        (back, ahead, far, wk, wv, gains, upper, lower, own["conv"])
    )
    other["conv"] = swap(conv_sent)
    row = jnp.stack([raw, back]), jnp.stack([jnp.concatenate(far, 0), ahead])
    first = turned(row[0], 1, 1), turned(row[1], 1, -1)
    stored = [stale_call(row, gains, wk, wv)]
    row, stored = lax.optimization_barrier((row, stored))
    second = turned(row[1], 1, 1), turned(row[0], 1, -1)
    far = turned(first[0], 1, 1), turned(first[1], 1, -1)
    stored.append(stale_call(first, gains, wk, wv))
    second, stored, sent = lax.optimization_barrier(
        (second, stored, {name: own[name] for name in ("query", "out")})
    )
    other |= {name: swap(value) for name, value in sent.items()}
    stored += [stale_call(pieces, gains, wk, wv) for pieces in (second, far)]

    x = lax.dynamic_index_in_dim(latent, core, 0, keepdims=False).reshape(CELLS, C)
    def two_blocks(x):
        return block_call(x, gains, conv_gains, upper, lower, own, other, stored)

    def hop(x):
        return lax.ppermute(x, "segment", [(i, i + 2) for i in range(6)])

    def chip_stage(stage, x):
        return lax.cond(stage < 3, hop, lambda x: x, two_blocks(x))

    x = lax.fori_loop(0, 4, chip_stage, x)

    groups = x.reshape(4, 4, 2, 8, C)
    keep = lax.dynamic_index_in_dim(groups, core, 2, keepdims=False)
    got = swap(lax.dynamic_index_in_dim(groups, 1 - core, 2, keepdims=False))
    both = jnp.stack(ordered(keep, got))
    result = jnp.where(lax.axis_index("segment") >= 6, both[:, :, 3], jnp.zeros_like(both[:, :, 3]))
    for d in (1, 2, 3):
        result = result + lax.ppermute(
            both[:, :, (3 + d) % 4], "segment", [(6, (6 + 2 * d) % 8), (7, (7 + 2 * d) % 8)]
        )
    return result.astype(F32)


def solution(mesh):
    in_specs = (
        P(None, "patch", None, None),
        P("segment", None, "patch", None, None),
        P("segment", None, "patch", None, None),
        P("segment", None),
        P("segment", None, None),
        P("segment", None, None),
        P("segment", None, None),
        P("segment", None, None),
        P("segment", None),
        P("segment", None, None, None, None),
    )
    out_specs = P(None, "patch", "segment", None)
    return jax.shard_map(shards, mesh=mesh, in_specs=in_specs, out_specs=out_specs, check_vma=False)
```

```python
import functools

import jax
import jax.numpy as jnp
from jax import lax
from jax.experimental import pallas as pl
from jax.experimental.pallas import tpu as pltpu
from jax.sharding import PartitionSpec as P

C = 640
PAIRS = 5
CELLS = 256
W = 64
KEYS = 4096
CHUNK = 2048
F32 = jnp.float32
BF = jnp.bfloat16
QSCALE = 0.125 * 1.4426950408889634


def normalize(values, gain):
    center = values - jnp.mean(values, axis=-1, keepdims=True)
    spread = jnp.mean(center * center, axis=-1, keepdims=True)
    return center * lax.rsqrt(spread + 1e-05) * gain


def dot(a, b):
    return jnp.dot(a, b, preferred_element_type=F32)


def dot_t(a, b):
    return lax.dot_general(a, b, (((1,), (1,)), ((), ())), preferred_element_type=F32)


def dot_turned(a, b):
    return lax.dot_general(a, b, (((0,), (1,)), ((), ())), preferred_element_type=F32)


def start_copy(use_own, own, other, target, sem):
    @pl.when(use_own)
    def _():
        pltpu.make_async_copy(own, target, sem).start()

    @pl.when(jnp.logical_not(use_own))
    def _():
        pltpu.make_async_copy(other, target, sem).start()


def wait_copy(own, target, sem):
    pltpu.make_async_copy(own, target, sem).wait()


def stale_kernel(near_ref, far_ref, ga_ref, wk_ref, wv_ref, k_ref, vt_ref):
    block = pl.program_id(0)
    raw = jnp.concatenate([near_ref[...], far_ref[...]], 0).reshape(-1, C).astype(F32)
    normed = normalize(raw, ga_ref[pl.ds(block, 1), :]).astype(BF)
    keys = dot(normed, wk_ref[...]).astype(BF)
    for pair in range(PAIRS):
        k_ref[pair] = keys[:, pair * 128 : (pair + 1) * 128]
    values = dot_turned(wv_ref[...], normed).astype(BF)
    for pair in range(PAIRS):
        vt_ref[pair] = values[pair * 128 : (pair + 1) * 128]


def stale_call(pieces, gains, wk, wv):
    size = pieces[0].shape[0]
    cells = 2 * size * CELLS
    return pl.pallas_call(
        stale_kernel,
        grid=(2,),
        out_shape=[
            jax.ShapeDtypeStruct((2, PAIRS, cells, 128), BF),
            jax.ShapeDtypeStruct((2, PAIRS, 128, cells), BF),
        ],
        in_specs=[
            pl.BlockSpec((size, None, CELLS, C), lambda b: (0, b, 0, 0)),
            pl.BlockSpec((size, None, CELLS, C), lambda b: (0, b, 0, 0)),
            pl.BlockSpec((2, C), lambda b: (0, 0)),
            pl.BlockSpec((None, C, C), lambda b: (b, 0, 0)),
            pl.BlockSpec((None, C, C), lambda b: (b, 0, 0)),
        ],
        out_specs=[
            pl.BlockSpec((None, PAIRS, cells, 128), lambda b: (b, 0, 0, 0)),
            pl.BlockSpec((None, PAIRS, 128, cells), lambda b: (b, 0, 0, 0)),
        ],
        compiler_params=pltpu.CompilerParams(vmem_limit_bytes=50 << 20),
        cost_estimate=pl.CostEstimate(
            flops=8 * cells * C * C, transcendentals=0, bytes_accessed=12 * cells * C
        ),
        name="stale",
    )(*pieces, gains, wk, wv)


STORES = 4
NAMES = ("query", "key", "value", "out", "conv")


def block_kernel(*refs):
    x_ref, ga_ref, gc_ref, up_ref, dn_ref = refs[:5]
    own = dict(zip(NAMES, refs[5:10]))
    other = dict(zip(NAMES, refs[10:15]))
    k_hbm, v_hbm = refs[15 : 15 + STORES], refs[15 + STORES : 15 + 2 * STORES]
    o_ref, wqk, wv, wout, wconv, keys, values = refs[15 + 2 * STORES : 22 + 2 * STORES]
    queries, fresh, fresh_t, context, mid, cols, sem_w, sem_k = refs[22 + 2 * STORES :]
    core = lax.axis_index("segment") % 2
    targets = {
        "query": wqk.at[:, pl.ds(0, C)],
        "key": wqk.at[:, pl.ds(C, C)],
        "value": wv,
        "out": wout,
        "conv": wconv,
    }

    def start(place, *names):
        for name in names:
            start_copy(
                core == place,
                own[name],
                other[name],
                targets[name],
                sem_w.at[NAMES.index(name)],
            )

    def wait(name):
        wait_copy(own[name], targets[name], sem_w.at[NAMES.index(name)])

    def pair_copies(place, pair):
        copies, begin = [], 0
        for i in range(STORES):
            size = k_hbm[i].shape[2]
            cells = pl.ds(begin, size)
            begin += size
            for source, target, j in (
                (k_hbm[i].at[place, pair], keys.at[pair, cells, :], i),
                (v_hbm[i].at[place, pair], values.at[pair, :, cells], STORES + i),
            ):
                copies.append(pltpu.make_async_copy(source, target, sem_k.at[pair, j]))
        return copies

    start(0, "query", "key", "value")
    for copy in pair_copies(0, 0):
        copy.start()
    mid[...] = x_ref[...].astype(F32)
    lane = lax.broadcasted_iota(jnp.int32, (CELLS, 128), 1)
    own_cells = pl.ds(0, CELLS)

    def one_block(place, _):
        def ahead(work):
            pl.when(place == 0)(work)

        normed = normalize(mid[...], ga_ref[pl.ds(place, 1), :]).astype(BF)
        for name in NAMES[:3]:
            wait(name)

        @pl.when(place == 0)
        def _():
            for pair in range(1, PAIRS):
                for copy in pair_copies(0, pair):
                    copy.start()
            start(0, "out", "conv")

        made = dot(normed, wqk[...])
        turned_values = dot_turned(wv[...], normed).astype(BF)
        for pair in range(PAIRS):
            lanes = slice(pair * 128, (pair + 1) * 128)
            queries[pair] = (made[:, lanes] * QSCALE).astype(BF)
            fresh[pair] = made[:, C + pair * 128 : C + (pair + 1) * 128].astype(BF)
            fresh_t[pair] = turned_values[lanes]
        ahead(lambda: start(1, "query", "key", "value"))

        def attend(pair):
            for copy in pair_copies(0, pair):
                copy.wait()
            keys[pair, own_cells, :] = fresh[pair]
            values[pair, :, own_cells] = fresh_t[pair]
            both = queries[pair]
            zero = jnp.zeros_like(both)
            heads = jnp.concatenate(
                [jnp.where(lane < 64, both, zero), jnp.where(lane < 64, zero, both)], 0
            )
            totals = jnp.zeros((8, 2 * CELLS), F32)
            sums = [jnp.zeros((64, CELLS), F32)] * 2
            for chunk in range(KEYS // CHUNK):
                cells = pl.ds(chunk * CHUNK, CHUNK)
                weights = jnp.exp2(dot_t(keys[pair, cells, :], heads))
                totals = totals + jnp.sum(weights.reshape(CHUNK // 8, 8, 2 * CELLS), 0)
                weights = weights.astype(BF)
                for head in range(2):
                    sums[head] = sums[head] + dot(
                        values[pair, head * 64 : (head + 1) * 64, cells],
                        weights[:, head * CELLS : (head + 1) * CELLS],
                    )
            totals = jnp.sum(totals, axis=0, keepdims=True)
            ready = [sums[i] / totals[:, i * CELLS : (i + 1) * CELLS] for i in range(2)]
            context[pair] = jnp.concatenate(ready, 0).T.astype(BF)

            def next_pair():
                for copy in pair_copies(1, pair):
                    copy.start()

            ahead(next_pair)

        for pair in range(PAIRS):
            attend(pair)

        wait("out")
        x_mid = mid[...] + dot(
            jnp.concatenate([context[pair] for pair in range(PAIRS)], 1), wout[...]
        )
        mid[...] = x_mid
        ahead(lambda: start(1, "out"))
        gated = normalize(x_mid, gc_ref[pl.ds(place, 1), :])
        gated = gated / (1.0 + jnp.exp(-gated))
        gated = gated.astype(BF).astype(F32)
        rows = CELLS + 2 * W
        extended = jnp.concatenate(
            [up_ref[place].astype(F32), gated, dn_ref[place].astype(F32)], 0
        )
        col = lax.broadcasted_iota(jnp.int32, (rows, C), 0) % W
        cols[0] = jnp.where(col == 0, 0.0, pltpu.roll(extended, 1, 0)).astype(BF)
        cols[1] = extended.astype(BF)
        cols[2] = jnp.where(col == W - 1, 0.0, pltpu.roll(extended, rows - 1, 0)).astype(BF)
        wait("conv")

        def tap_row(i, _):
            cells = pl.ds(pl.multiple_of(i * W, W), CELLS)
            total = mid[...]
            for j in range(3):
                total = total + dot(cols[j, cells, :], wconv[3 * i + j])
            mid[...] = total
            return 0

        lax.fori_loop(0, 3, tap_row, 0)
        ahead(lambda: start(1, "conv"))
        return 0

    lax.fori_loop(0, 2, one_block, 0)
    o_ref[...] = mid[...].astype(o_ref.dtype)


def block_call(x, gain_attn, gain_conv, up, down, own, other, stored):
    vmem = pl.BlockSpec(memory_space=pltpu.VMEM)
    hbm = pl.BlockSpec(memory_space=pltpu.HBM)
    return pl.pallas_call(
        block_kernel,
        out_shape=jax.ShapeDtypeStruct((CELLS, C), BF),
        in_specs=[vmem] * 5 + [hbm] * (10 + 2 * STORES),
        out_specs=vmem,
        scratch_shapes=[
            pltpu.VMEM((C, 2 * C), BF),
            pltpu.VMEM((C, C), BF),
            pltpu.VMEM((C, C), BF),
            pltpu.VMEM((9, C, C), BF),
            pltpu.VMEM((PAIRS, KEYS, 128), BF),
            pltpu.VMEM((PAIRS, 128, KEYS), BF),
            pltpu.VMEM((PAIRS, CELLS, 128), BF),
            pltpu.VMEM((PAIRS, CELLS, 128), BF),
            pltpu.VMEM((PAIRS, 128, CELLS), BF),
            pltpu.VMEM((PAIRS, CELLS, 128), BF),
            pltpu.VMEM((CELLS, C), F32),
            pltpu.VMEM((3, CELLS + 2 * W, C), BF),
            pltpu.SemaphoreType.DMA((5,)),
            pltpu.SemaphoreType.DMA((PAIRS, 2 * STORES)),
        ],
        compiler_params=pltpu.CompilerParams(vmem_limit_bytes=58 << 20),
        cost_estimate=pl.CostEstimate(
            flops=2 * 13_000_000_000,
            transcendentals=2 * 10_500_000,
            bytes_accessed=2 * 22_000_000,
        ),
        name="blocks",
    )(
        x,
        gain_attn,
        gain_conv,
        up,
        down,
        *[own[name] for name in NAMES],
        *[other[name] for name in NAMES],
        *[pair[0] for pair in stored],
        *[pair[1] for pair in stored],
    )


def turned(value, leg, by):
    pairs = []
    for segment in range(8):
        for y in range(4):
            for z in range(4):
                if segment % 2 == leg:
                    to = y, (z + by) % 4
                else:
                    to = (y + by) % 4, z
                pairs.append((16 * segment + 4 * y + z, 16 * segment + 4 * to[0] + to[1]))
    return lax.ppermute(value, ("segment", "patch"), pairs)


def ring_near(value, leg):
    return turned(value, leg, 1), turned(value, leg, -1)


def ring_far(back, ahead, leg):
    half = back.shape[0] // 2
    return turned(back[:half], leg, 1), turned(ahead[half:], leg, -1)


def shards(
    latent, stale_attn, stale_edge, norm_attn, query_w, key_w, value_w, out_w, norm_conv, conv_w
):
    core = lax.axis_index("segment") % 2
    is_first = core == 0
    sibling = [(i, i ^ 1) for i in range(8)]

    def swap(value):
        return lax.ppermute(value, "segment", sibling)

    def ordered(own, other):
        return jnp.where(is_first, own, other), jnp.where(is_first, other, own)

    def exchanged(value):
        keep = lax.dynamic_index_in_dim(value, core, 0, keepdims=False)
        give = lax.dynamic_index_in_dim(value, 1 - core, 0, keepdims=False)
        return ordered(keep, swap(give))

    own = dict(zip(NAMES, (query_w[0], key_w[0], value_w[0], out_w[0], conv_w[0].reshape(9, C, C))))
    mine = jnp.concatenate(
        [stale_attn[0].reshape(2, CELLS, C), stale_edge[0].reshape(2, 2 * W, C)], 1
    )
    mine = jnp.stack(exchanged(mine))
    raw, edges = mine[:, :CELLS], mine[:, CELLS:].reshape(2, 2, W, C)
    gains = jnp.concatenate(ordered(norm_attn, swap(norm_attn)), 0)
    conv_gains = jnp.concatenate(ordered(norm_conv, swap(norm_conv)), 0)
    raw, sent = lax.optimization_barrier(
        (raw, {name: own[name] for name in ("key", "value")})
    )
    other = {name: swap(value) for name, value in sent.items()}
    wk, wv = [jnp.stack(ordered(own[name], other[name])) for name in ("key", "value")]
    back, ahead = ring_near(raw, 0)
    far = ring_far(back, ahead, 0)
    back, ahead, far, wk, wv, gains, sent = lax.optimization_barrier(
        (back, ahead, far, wk, wv, gains, own["conv"])
    )
    other["conv"] = swap(sent)
    row = jnp.stack([raw, back]), jnp.stack([jnp.concatenate(far, 0), ahead])
    first = turned(row[0], 1, 1), turned(row[1], 1, -1)
    stored = [stale_call(row, gains, wk, wv)]
    row, stored = lax.optimization_barrier((row, stored))
    second = turned(row[1], 1, 1), turned(row[0], 1, -1)
    far = turned(first[0], 1, 1), turned(first[1], 1, -1)
    stored.append(stale_call(first, gains, wk, wv))
    second, stored, edges = lax.optimization_barrier((second, stored, edges))
    upper = lax.ppermute(edges[:, 1], "patch", [(i, i + 1) for i in range(15)])
    lower = lax.ppermute(edges[:, 0], "patch", [(i + 1, i) for i in range(15)])
    stored.append(stale_call(second, gains, wk, wv))
    far, upper, lower, stored, sent = lax.optimization_barrier(
        (far, upper, lower, stored, {name: own[name] for name in ("query", "out")})
    )
    other |= {name: swap(value) for name, value in sent.items()}
    stored.append(stale_call(far, gains, wk, wv))

    x = lax.dynamic_index_in_dim(latent, core, 0, keepdims=False).reshape(CELLS, C)
    def two_blocks(x):
        return block_call(x, gains, conv_gains, upper, lower, own, other, stored)

    def hop(x):
        return lax.ppermute(x, "segment", [(i, i + 2) for i in range(6)])

    def chip_stage(stage, x):
        return lax.cond(stage < 3, hop, lambda x: x, two_blocks(x))

    x = lax.fori_loop(0, 4, chip_stage, x)

    groups = x.reshape(4, 4, 2, 8, C)
    keep = lax.dynamic_index_in_dim(groups, core, 2, keepdims=False)
    got = swap(lax.dynamic_index_in_dim(groups, 1 - core, 2, keepdims=False))
    both = jnp.stack(ordered(keep, got))
    result = jnp.where(lax.axis_index("segment") >= 6, both[:, :, 3], jnp.zeros_like(both[:, :, 3]))
    for d in (1, 2, 3):
        result = result + lax.ppermute(
            both[:, :, (3 + d) % 4], "segment", [(6, (6 + 2 * d) % 8), (7, (7 + 2 * d) % 8)]
        )
    return result.astype(F32)


def solution(mesh):
    in_specs = (
        P(None, "patch", None, None),
        P("segment", None, "patch", None, None),
        P("segment", None, "patch", None, None),
        P("segment", None),
        P("segment", None, None),
        P("segment", None, None),
        P("segment", None, None),
        P("segment", None, None),
        P("segment", None),
        P("segment", None, None, None, None),
    )
    out_specs = P(None, "patch", "segment", None)
    return jax.shard_map(shards, mesh=mesh, in_specs=in_specs, out_specs=out_specs, check_vma=False)
```

```python
import functools

import jax
import jax.numpy as jnp
from jax import lax
from jax.experimental import pallas as pl
from jax.experimental.pallas import tpu as pltpu
from jax.sharding import PartitionSpec as P

C = 640
PAIRS = 5
CELLS = 256
W = 64
KEYS = 4096
CHUNK = 2048
F32 = jnp.float32
BF = jnp.bfloat16
QSCALE = 0.125 * 1.4426950408889634


def normalize(values, gain):
    center = values - jnp.mean(values, axis=-1, keepdims=True)
    spread = jnp.mean(center * center, axis=-1, keepdims=True)
    return center * lax.rsqrt(spread + 1e-05) * gain


def dot(a, b):
    return jnp.dot(a, b, preferred_element_type=F32)


def dot_t(a, b):
    return lax.dot_general(a, b, (((1,), (1,)), ((), ())), preferred_element_type=F32)


def dot_turned(a, b):
    return lax.dot_general(a, b, (((0,), (1,)), ((), ())), preferred_element_type=F32)


def start_copy(use_own, own, other, target, sem):
    @pl.when(use_own)
    def _():
        pltpu.make_async_copy(own, target, sem).start()

    @pl.when(jnp.logical_not(use_own))
    def _():
        pltpu.make_async_copy(other, target, sem).start()


def wait_copy(own, target, sem):
    pltpu.make_async_copy(own, target, sem).wait()


def stale_kernel(near_ref, far_ref, ga_ref, wk_ref, wv_ref, k_ref, vt_ref):
    block = pl.program_id(0)
    raw = jnp.concatenate([near_ref[...], far_ref[...]], 0).reshape(-1, C).astype(F32)
    normed = normalize(raw, ga_ref[pl.ds(block, 1), :]).astype(BF)
    keys = dot(normed, wk_ref[...]).astype(BF)
    for pair in range(PAIRS):
        k_ref[pair] = keys[:, pair * 128 : (pair + 1) * 128]
    values = dot_turned(wv_ref[...], normed).astype(BF)
    for pair in range(PAIRS):
        vt_ref[pair] = values[pair * 128 : (pair + 1) * 128]


def stale_call(pieces, gains, wk, wv):
    size = pieces[0].shape[0]
    cells = 2 * size * CELLS
    return pl.pallas_call(
        stale_kernel,
        grid=(2,),
        out_shape=[
            jax.ShapeDtypeStruct((2, PAIRS, cells, 128), BF),
            jax.ShapeDtypeStruct((2, PAIRS, 128, cells), BF),
        ],
        in_specs=[
            pl.BlockSpec((size, None, CELLS, C), lambda b: (0, b, 0, 0)),
            pl.BlockSpec((size, None, CELLS, C), lambda b: (0, b, 0, 0)),
            pl.BlockSpec((2, C), lambda b: (0, 0)),
            pl.BlockSpec((None, C, C), lambda b: (b, 0, 0)),
            pl.BlockSpec((None, C, C), lambda b: (b, 0, 0)),
        ],
        out_specs=[
            pl.BlockSpec((None, PAIRS, cells, 128), lambda b: (b, 0, 0, 0)),
            pl.BlockSpec((None, PAIRS, 128, cells), lambda b: (b, 0, 0, 0)),
        ],
        compiler_params=pltpu.CompilerParams(vmem_limit_bytes=50 << 20),
        cost_estimate=pl.CostEstimate(
            flops=8 * cells * C * C, transcendentals=0, bytes_accessed=12 * cells * C
        ),
        name="stale",
    )(*pieces, gains, wk, wv)


STORES = 4
NAMES = ("query", "key", "value", "out", "conv")


def block_kernel(*refs):
    x_ref, ga_ref, gc_ref, up_ref, dn_ref = refs[:5]
    own = dict(zip(NAMES, refs[5:10]))
    other = dict(zip(NAMES, refs[10:15]))
    k_hbm, v_hbm = refs[15 : 15 + STORES], refs[15 + STORES : 15 + 2 * STORES]
    o_ref, wqk, wv, wout, wconv, keys, values = refs[15 + 2 * STORES : 22 + 2 * STORES]
    queries, fresh, fresh_t, context, mid, cols, sem_w, sem_k = refs[22 + 2 * STORES :]
    core = lax.axis_index("segment") % 2
    targets = {
        "query": wqk.at[:, pl.ds(0, C)],
        "key": wqk.at[:, pl.ds(C, C)],
        "value": wv,
        "out": wout,
        "conv": wconv,
    }

    def start(place, *names):
        for name in names:
            start_copy(
                core == place,
                own[name],
                other[name],
                targets[name],
                sem_w.at[NAMES.index(name)],
            )

    def wait(name):
        wait_copy(own[name], targets[name], sem_w.at[NAMES.index(name)])

    def pair_copies(place, pair):
        copies, begin = [], 0
        for i in range(STORES):
            size = k_hbm[i].shape[2]
            cells = pl.ds(begin, size)
            begin += size
            for source, target, j in (
                (k_hbm[i].at[place, pair], keys.at[pair, cells, :], i),
                (v_hbm[i].at[place, pair], values.at[pair, :, cells], STORES + i),
            ):
                copies.append(pltpu.make_async_copy(source, target, sem_k.at[pair, j]))
        return copies

    start(0, "query", "key", "value")
    for copy in pair_copies(0, 0):
        copy.start()
    mid[...] = x_ref[...].astype(F32)
    lane = lax.broadcasted_iota(jnp.int32, (CELLS, 128), 1)
    own_cells = pl.ds(0, CELLS)

    def one_block(place, _):
        def ahead(work):
            pl.when(place == 0)(work)

        normed = normalize(mid[...], ga_ref[pl.ds(place, 1), :]).astype(BF)
        for name in NAMES[:3]:
            wait(name)

        @pl.when(place == 0)
        def _():
            for pair in range(1, PAIRS):
                for copy in pair_copies(0, pair):
                    copy.start()
            start(0, "out", "conv")

        made = dot(normed, wqk[...])
        turned_values = dot_turned(wv[...], normed).astype(BF)
        for pair in range(PAIRS):
            lanes = slice(pair * 128, (pair + 1) * 128)
            queries[pair] = (made[:, lanes] * QSCALE).astype(BF)
            fresh[pair] = made[:, C + pair * 128 : C + (pair + 1) * 128].astype(BF)
            fresh_t[pair] = turned_values[lanes]
        ahead(lambda: start(1, "query", "key", "value"))

        def attend(pair):
            for copy in pair_copies(0, pair):
                copy.wait()
            keys[pair, own_cells, :] = fresh[pair]
            values[pair, :, own_cells] = fresh_t[pair]
            both = queries[pair]
            zero = jnp.zeros_like(both)
            heads = jnp.concatenate(
                [jnp.where(lane < 64, both, zero), jnp.where(lane < 64, zero, both)], 0
            )
            totals = jnp.zeros((8, 2 * CELLS), F32)
            sums = [jnp.zeros((64, CELLS), F32)] * 2
            for chunk in range(KEYS // CHUNK):
                cells = pl.ds(chunk * CHUNK, CHUNK)
                weights = jnp.exp2(dot_t(keys[pair, cells, :], heads))
                totals = totals + jnp.sum(weights.reshape(CHUNK // 8, 8, 2 * CELLS), 0)
                weights = weights.astype(BF)
                for head in range(2):
                    sums[head] = sums[head] + dot(
                        values[pair, head * 64 : (head + 1) * 64, cells],
                        weights[:, head * CELLS : (head + 1) * CELLS],
                    )
            totals = jnp.sum(totals, axis=0, keepdims=True)
            ready = [sums[i] / totals[:, i * CELLS : (i + 1) * CELLS] for i in range(2)]
            context[pair] = jnp.concatenate(ready, 0).T.astype(BF)

            def next_pair():
                for copy in pair_copies(1, pair):
                    copy.start()

            ahead(next_pair)

        for pair in range(PAIRS):
            attend(pair)

        wait("out")
        x_mid = mid[...] + dot(
            jnp.concatenate([context[pair] for pair in range(PAIRS)], 1), wout[...]
        )
        mid[...] = x_mid
        ahead(lambda: start(1, "out"))
        gated = normalize(x_mid, gc_ref[pl.ds(place, 1), :])
        gated = gated / (1.0 + jnp.exp(-gated))
        gated = gated.astype(BF).astype(F32)
        rows = CELLS + 2 * W
        extended = jnp.concatenate(
            [up_ref[place].astype(F32), gated, dn_ref[place].astype(F32)], 0
        )
        col = lax.broadcasted_iota(jnp.int32, (rows, C), 0) % W
        cols[0] = jnp.where(col == 0, 0.0, pltpu.roll(extended, 1, 0)).astype(BF)
        cols[1] = extended.astype(BF)
        cols[2] = jnp.where(col == W - 1, 0.0, pltpu.roll(extended, rows - 1, 0)).astype(BF)
        wait("conv")

        def tap_row(i, _):
            cells = pl.ds(pl.multiple_of(i * W, W), CELLS)
            total = mid[...]
            for j in range(3):
                total = total + dot(cols[j, cells, :], wconv[3 * i + j])
            mid[...] = total
            return 0

        lax.fori_loop(0, 3, tap_row, 0)
        ahead(lambda: start(1, "conv"))
        return 0

    lax.fori_loop(0, 2, one_block, 0)
    o_ref[...] = mid[...].astype(o_ref.dtype)


def block_call(x, gain_attn, gain_conv, up, down, own, other, stored):
    vmem = pl.BlockSpec(memory_space=pltpu.VMEM)
    hbm = pl.BlockSpec(memory_space=pltpu.HBM)
    return pl.pallas_call(
        block_kernel,
        out_shape=jax.ShapeDtypeStruct((CELLS, C), BF),
        in_specs=[vmem] * 5 + [hbm] * (10 + 2 * STORES),
        out_specs=vmem,
        scratch_shapes=[
            pltpu.VMEM((C, 2 * C), BF),
            pltpu.VMEM((C, C), BF),
            pltpu.VMEM((C, C), BF),
            pltpu.VMEM((9, C, C), BF),
            pltpu.VMEM((PAIRS, KEYS, 128), BF),
            pltpu.VMEM((PAIRS, 128, KEYS), BF),
            pltpu.VMEM((PAIRS, CELLS, 128), BF),
            pltpu.VMEM((PAIRS, CELLS, 128), BF),
            pltpu.VMEM((PAIRS, 128, CELLS), BF),
            pltpu.VMEM((PAIRS, CELLS, 128), BF),
            pltpu.VMEM((CELLS, C), F32),
            pltpu.VMEM((3, CELLS + 2 * W, C), BF),
            pltpu.SemaphoreType.DMA((5,)),
            pltpu.SemaphoreType.DMA((PAIRS, 2 * STORES)),
        ],
        compiler_params=pltpu.CompilerParams(vmem_limit_bytes=58 << 20),
        cost_estimate=pl.CostEstimate(
            flops=2 * 13_000_000_000,
            transcendentals=2 * 10_500_000,
            bytes_accessed=2 * 22_000_000,
        ),
        name="blocks",
    )(
        x,
        gain_attn,
        gain_conv,
        up,
        down,
        *[own[name] for name in NAMES],
        *[other[name] for name in NAMES],
        *[pair[0] for pair in stored],
        *[pair[1] for pair in stored],
    )


def turned(value, leg, by):
    pairs = []
    for segment in range(8):
        for y in range(4):
            for z in range(4):
                if segment % 2 == leg:
                    to = y, (z + by) % 4
                else:
                    to = (y + by) % 4, z
                pairs.append((16 * segment + 4 * y + z, 16 * segment + 4 * to[0] + to[1]))
    return lax.ppermute(value, ("segment", "patch"), pairs)


def ring_near(value, leg):
    return turned(value, leg, 1), turned(value, leg, -1)


def ring_far(back, ahead, leg):
    half = back.shape[0] // 2
    return turned(back[:half], leg, 1), turned(ahead[half:], leg, -1)


def shards(
    latent, stale_attn, stale_edge, norm_attn, query_w, key_w, value_w, out_w, norm_conv, conv_w
):
    core = lax.axis_index("segment") % 2
    is_first = core == 0
    sibling = [(i, i ^ 1) for i in range(8)]

    def swap(value):
        return lax.ppermute(value, "segment", sibling)

    def ordered(own, other):
        return jnp.where(is_first, own, other), jnp.where(is_first, other, own)

    def exchanged(value):
        keep = lax.dynamic_index_in_dim(value, core, 0, keepdims=False)
        give = lax.dynamic_index_in_dim(value, 1 - core, 0, keepdims=False)
        return ordered(keep, swap(give))

    own = dict(zip(NAMES, (query_w[0], key_w[0], value_w[0], out_w[0], conv_w[0].reshape(9, C, C))))
    mine = jnp.concatenate(
        [stale_attn[0].reshape(2, CELLS, C), stale_edge[0].reshape(2, 2 * W, C)], 1
    )
    mine = jnp.stack(exchanged(mine))
    raw, edges = mine[:, :CELLS], mine[:, CELLS:].reshape(2, 2, W, C)
    gains = jnp.concatenate(ordered(norm_attn, swap(norm_attn)), 0)
    conv_gains = jnp.concatenate(ordered(norm_conv, swap(norm_conv)), 0)
    raw, sent = lax.optimization_barrier(
        (raw, {name: own[name] for name in ("key", "value")})
    )
    other = {name: swap(value) for name, value in sent.items()}
    wk, wv = [jnp.stack(ordered(own[name], other[name])) for name in ("key", "value")]
    back, ahead = ring_near(raw, 0)
    far = ring_far(back, ahead, 0)
    back, ahead, far, wk, wv, gains, sent = lax.optimization_barrier(
        (back, ahead, far, wk, wv, gains, own["conv"])
    )
    other["conv"] = swap(sent)
    row = jnp.stack([raw, back]), jnp.stack([jnp.concatenate(far, 0), ahead])
    first = turned(row[0], 1, 1), turned(row[1], 1, -1)
    stored = [stale_call(row, gains, wk, wv)]
    second = turned(row[1], 1, 1), turned(row[0], 1, -1)
    first, stored = lax.optimization_barrier((first, stored))
    far = turned(first[0], 1, 1), turned(first[1], 1, -1)
    stored.append(stale_call(first, gains, wk, wv))
    second, stored, edges = lax.optimization_barrier((second, stored, edges))
    upper = lax.ppermute(edges[:, 1], "patch", [(i, i + 1) for i in range(15)])
    lower = lax.ppermute(edges[:, 0], "patch", [(i + 1, i) for i in range(15)])
    stored.append(stale_call(second, gains, wk, wv))
    far, upper, lower, stored, sent = lax.optimization_barrier(
        (far, upper, lower, stored, {name: own[name] for name in ("query", "out")})
    )
    other |= {name: swap(value) for name, value in sent.items()}
    stored.append(stale_call(far, gains, wk, wv))

    x = lax.dynamic_index_in_dim(latent, core, 0, keepdims=False).reshape(CELLS, C)
    def two_blocks(x):
        return block_call(x, gains, conv_gains, upper, lower, own, other, stored)

    def hop(x):
        return lax.ppermute(x, "segment", [(i, i + 2) for i in range(6)])

    def chip_stage(stage, x):
        return lax.cond(stage < 3, hop, lambda x: x, two_blocks(x))

    x = lax.fori_loop(0, 4, chip_stage, x)

    groups = x.reshape(4, 4, 2, 8, C)
    keep = lax.dynamic_index_in_dim(groups, core, 2, keepdims=False)
    got = swap(lax.dynamic_index_in_dim(groups, 1 - core, 2, keepdims=False))
    both = jnp.stack(ordered(keep, got))
    result = jnp.where(lax.axis_index("segment") >= 6, both[:, :, 3], jnp.zeros_like(both[:, :, 3]))
    for d in (1, 2, 3):
        result = result + lax.ppermute(
            both[:, :, (3 + d) % 4], "segment", [(6, (6 + 2 * d) % 8), (7, (7 + 2 * d) % 8)]
        )
    return result.astype(F32)


def solution(mesh):
    in_specs = (
        P(None, "patch", None, None),
        P("segment", None, "patch", None, None),
        P("segment", None, "patch", None, None),
        P("segment", None),
        P("segment", None, None),
        P("segment", None, None),
        P("segment", None, None),
        P("segment", None, None),
        P("segment", None),
        P("segment", None, None, None, None),
    )
    out_specs = P(None, "patch", "segment", None)
    return jax.shard_map(shards, mesh=mesh, in_specs=in_specs, out_specs=out_specs, check_vma=False)
```
